128 devices in a mesh: aux: 128 (over y, x, z, core).
Axes of the slice: x: 4, y: 4, z: 4, core: 2. Of those that a mesh axis runs over, the one named last changes fastest.
Arguments:
- state: float32 [128, 2, 256, 256], P('aux'), may hold values from -6 to 6
- h_static: float32 [2, 256, 256], replicated, may hold values from -0.375 to 0.375
- drive_op: float32 [2, 256, 256], replicated, may hold values from -0.375 to 0.375
- couple: float32 [3, 256, 256], replicated, may hold values from -0.375 to 0.375
- bath_coef: float32 [2, 3], replicated, may hold values from -2 to 2
- damping: float32 [3], replicated, may hold values from 0.3 to 3
- occupation: int32 [128, 3], P('aux'), may hold values from 1 to 3
- raise_nbr: int32 [128, 3], P('aux'), may hold values from -1 to 127, as said below
- lower_nbr: int32 [128, 3], P('aux'), may hold values from -1 to 127, as said below
Outputs:
- new_state: float32 [128, 2, 256, 256], P('aux')
The draws below stay inside these ranges and needn't reach their ends.
Inputs may be any that keep to these rules, and one draw needn't show every extreme that they name: `raise_nbr`: each entry is -1 or the index of an auxiliary matrix held on a device 1 to 2 after its own holder (auxiliary a is held by device a); the first mode's entry is -1 only on the last 2 devices. `lower_nbr`: each entry is -1 or the index of an auxiliary matrix held on a device 1 to 2 before its own holder (auxiliary a is held by device a); the first mode's entry is -1 only on the first 2 devices.
All inputs are finite; a program needn't handle non-finite values.
Results may differ from the reference program's by a relative error of at most 0.0003.
Values sent between devices are 32-bit elements; how exact they have to be, the bound alone decides.
A program may use at most 64 MiB of HBM per device.

```python
import math
import jax
import jax.numpy as jnp
from jax import lax

M = 256
MODES = 3
SPAN = 2
AUX_DEV = 1
AUXILIARIES = 128


def neighbour_list(key, sign):
    key_off, key_rot, key_slot, key_keep = jax.random.split(key, 4)
    holder = jnp.arange(AUXILIARIES, dtype=jnp.int32) // AUX_DEV
    offsets = jax.random.randint(key_off, (AUXILIARIES, MODES), 1, SPAN + 1)
    rotation = jax.random.randint(key_rot, (), 0, SPAN)
    first_col = 1 + (holder + rotation) % SPAN
    offsets = offsets.at[:, 0].set(first_col)
    slots = jax.random.randint(key_slot, (AUXILIARIES, MODES), 0, AUX_DEV)
    keeper = jax.random.randint(key_keep, (AUXILIARIES, MODES), 0, 8) > 0
    keeper = keeper.at[:, 0].set(True)
    device_of = holder[:, None] + sign * offsets
    target = device_of * AUX_DEV + slots
    usable = keeper & (device_of >= 0) & (device_of < AUXILIARIES // AUX_DEV)
    return jnp.where(usable, target, -1).astype(jnp.int32)


def draw_raise_nbr(key, part):
    return neighbour_list(jax.random.fold_in(key, 11), 1)


def draw_lower_nbr(key, part):
    return neighbour_list(jax.random.fold_in(key, 23), -1)


def place_ends(drawn, key, low, top_value):
    index_at = [jax.random.randint(jax.random.fold_in(key, axis), (), 0, length) for axis, length in enumerate(drawn.shape)]
    longest = drawn.shape.index(max(drawn.shape))
    beside = index_at[:longest] + [(index_at[longest] + 1) % drawn.shape[longest]] + index_at[longest + 1:]
    return drawn.at[tuple(index_at)].set(low).at[tuple(beside)].set(top_value)


def level_of(stream_key, extent, shards, least, top_value):
    loudness = 1.0
    for dim, shards_of in shards:
        heights = jax.random.uniform(jax.random.fold_in(jax.random.fold_in(stream_key, 6), dim), (shards_of,), jnp.float32, least / len(shards), top_value / len(shards))
        loudness = loudness * jnp.repeat(jnp.exp(heights), extent[dim] // shards_of).reshape((-1,) + (1,) * (len(extent) - 1 - dim))
    return loudness


def scatter_about(rng, shape, spread, most, pieces=(), held_as=jnp.bfloat16):
    gain = level_of(rng, shape, pieces, -0.22, 0.18) if pieces else 1.0
    values = jax.random.normal(rng, shape, jnp.float32) * spread * gain
    return jnp.minimum(jnp.maximum(values, -most), most).astype(held_as)


def setup_inputs(seed: int = 0) -> dict:
    key_list = jax.random.split(jax.random.key(seed), 10)
    return {
        "state": scatter_about(key_list[0], (AUXILIARIES, 2, M, M), 1.0, 6.0, ((0, 128),), jnp.float32),
        "h_static": scatter_about(key_list[1], (2, M, M), M ** -0.5, 0.375, (), jnp.float32),
        "drive_op": scatter_about(key_list[2], (2, M, M), M ** -0.5, 0.375, (), jnp.float32),
        "couple": scatter_about(key_list[3], (MODES, M, M), M ** -0.5, 0.375, (), jnp.float32),
        "bath_coef": jnp.clip(jax.random.uniform(key_list[4], (2, MODES), jnp.float32, -2.0, 2.0), -2.0, 2.0),
        "damping": jnp.clip(jnp.exp(jax.random.uniform(key_list[5], (MODES,), jnp.float32, math.log(0.3), math.log(3.0))), 0.3, 3.0),
        "occupation": place_ends(jax.random.randint(key_list[6], (AUXILIARIES, MODES), 1, 4), jax.random.fold_in(key_list[6], 1), 1, 3).astype(jnp.int32),
        "raise_nbr": draw_raise_nbr(jax.random.fold_in(key_list[9], 71), 0),
        "lower_nbr": draw_lower_nbr(jax.random.fold_in(key_list[9], 71), 0),
    }


HIGH = lax.Precision.HIGHEST
time_step = 0.05
drive_amp = 2.0
drive_freq = 20.0


def mul_left(matrix, batch):
    return jnp.einsum("ij,bjk->bik", matrix, batch, precision=HIGH)


def mul_right(batch, matrix):
    return jnp.einsum("bij,jk->bik", batch, matrix, precision=HIGH)


def hamil_comm(h_re, h_im, block):
    x_real = block[:, 0]
    x_imag = block[:, 1]
    comm_re = mul_left(h_re, x_real) - mul_left(h_im, x_imag) - mul_right(x_real, h_re) + mul_right(x_imag, h_im)
    comm_im = mul_left(h_re, x_imag) + mul_left(h_im, x_real) - mul_right(x_real, h_im) - mul_right(x_imag, h_re)
    return jnp.stack([comm_im, -comm_re], axis=1)


def derivative(block, raised, lowered, h_re, h_im, coupling, bath_coef, damping, level_counts):
    local_count = block.shape[0]
    rates = jnp.sum(level_counts * damping[None, :], axis=1)
    total = hamil_comm(h_re, h_im, block) - rates[:, None, None, None] * block
    for mode in range(coupling.shape[0]):
        stacked = jnp.concatenate([raised[:, mode], lowered[:, mode]], axis=0)
        flat = stacked.reshape((-1,) + stacked.shape[2:])
        q_times = mul_left(coupling[mode], flat).reshape(stacked.shape)
        times_q = mul_right(flat, coupling[mode]).reshape(stacked.shape)
        up_diff = q_times[:local_count] - times_q[:local_count]
        total = total + jnp.stack([up_diff[:, 1], -up_diff[:, 0]], axis=1)
        low_sum = q_times[local_count:] + times_q[local_count:]
        low_diff = q_times[local_count:] - times_q[local_count:]
        coef_re = bath_coef[0, mode]
        coef_im = bath_coef[1, mode]
        weight_n = level_counts[:, mode][:, None, None]
        part_re = weight_n * (coef_im * low_sum[:, 0] + coef_re * low_diff[:, 1])
        part_im = weight_n * (coef_im * low_sum[:, 1] - coef_re * low_diff[:, 0])
        total = total + jnp.stack([part_re, part_im], axis=1)
    return total


def reference(state, h_static, drive_op, couple, bath_coef, damping, occupation, raise_nbr, lower_nbr):
    h0_re = (h_static[0] + h_static[0].T) / 2
    h0_im = (h_static[1] - h_static[1].T) / 2
    dv_re = (drive_op[0] + drive_op[0].T) / 2
    dv_im = (drive_op[1] - drive_op[1].T) / 2
    coupling = (couple + jnp.swapaxes(couple, 1, 2)) / 2
    levels = occupation.astype(jnp.float32)

    def field(section_in, moment):
        drive_now = drive_amp * jnp.cos(jnp.float32(drive_freq * moment))
        h_re = h0_re + drive_now * dv_re
        h_im = h0_im + drive_now * dv_im

        def single(entries):
            block, up_list, down_list, level_row = entries
            up_ok = up_list >= 0
            down_ok = down_list >= 0
            raised = jnp.take(section_in, jnp.where(up_ok, up_list, 0).astype(jnp.int32), axis=0)
            raised = jnp.where(up_ok[:, None, None, None], raised, jnp.float32(0.0))
            lowered = jnp.take(section_in, jnp.where(down_ok, down_list, 0).astype(jnp.int32), axis=0)
            lowered = jnp.where(down_ok[:, None, None, None], lowered, jnp.float32(0.0))
            return derivative(block[None], raised[None], lowered[None], h_re, h_im, coupling, bath_coef, damping, level_row[None])[0]

        return lax.map(single, (section_in, raise_nbr, lower_nbr, levels))

    half = time_step / 2
    first = field(state, 0.0)
    second = field(state + half * first, half)
    third = field(state + half * second, half)
    fourth = field(state + time_step * third, time_step)
    return state + (time_step / 6) * (first + 2 * second + 2 * third + fourth)
```

```python
import functools

import jax
import jax.numpy as jnp
import numpy as np
from jax import lax
from jax.experimental import pallas as pl
from jax.experimental.pallas import tpu as pltpu
from jax.sharding import PartitionSpec as P

MESH = pl.DeviceIdType.MESH
STEP = 0.05
AMP = 2.0
FREQ = 20.0
M = 256
MODES = 3
STAGES = 4
SIB, FAR, NEAR, BACK, OWN = range(5)
RE, IM = 0, 1
BF = jnp.bfloat16
F32 = jnp.float32


def split(value):
    high = value.astype(BF)
    return high, (value - high.astype(F32)).astype(BF)


def kernel(
    count,
    bath,
    damp,
    occ,
    up,
    down,
    state,
    h_static,
    drive_op,
    couple,
    out,
    ybuf,
    win,
    raw,
    herm,
    left_of,
    right_of,
    total,
    acc,
    load_sem,
    send_sem,
    recv_sem,
):
    me = lax.axis_index("aux")
    odd = lax.rem(me, 2)
    d = 1 - 2 * odd

    def at(offset):
        return lax.rem(me + offset + count, count)

    partner = [at(d), at(2 * d), at(-d), at(-2 * d)]

    loads = [
        pltpu.make_async_copy(state.at[0], ybuf.at[0], load_sem.at[0]),
        pltpu.make_async_copy(couple, raw.at[pl.ds(0, 3)], load_sem.at[1]),
        pltpu.make_async_copy(h_static, raw.at[pl.ds(3, 2)], load_sem.at[2]),
        pltpu.make_async_copy(drive_op, raw.at[pl.ds(5, 2)], load_sem.at[3]),
    ]
    for load in loads:
        load.start()

    barrier = pltpu.get_barrier_semaphore()
    for other in partner:
        pl.semaphore_signal(barrier, inc=1, device_id=(other,), device_id_type=MESH)
    pl.semaphore_wait(barrier, 4)

    def remote(src, stage, to_slot, plane, number, device):
        return pltpu.make_async_remote_copy(
            src_ref=src,
            dst_ref=win.at[stage, to_slot, plane],
            send_sem=send_sem.at[stage, number],
            recv_sem=recv_sem.at[stage, to_slot, plane],
            device_id=(device,),
            device_id_type=MESH,
        )

    def own_sends(stage):
        own = ybuf.at[stage]
        return [
            remote(own.at[RE], stage, FAR, RE, 0, partner[BACK]),
            remote(own.at[IM], stage, NEAR, IM, 1, partner[NEAR]),
            remote(own.at[RE], stage, BACK, RE, 2, partner[FAR]),
            remote(own.at[IM], stage, BACK, IM, 3, partner[FAR]),
            remote(own.at[RE], stage, SIB, RE, 4, partner[SIB]),
            remote(own.at[IM], stage, SIB, IM, 5, partner[SIB]),
        ]

    def forwards(stage):
        return [
            remote(win.at[stage, FAR, RE], stage, NEAR, RE, 6, partner[SIB]),
            remote(win.at[stage, NEAR, IM], stage, FAR, IM, 7, partner[SIB]),
        ]

    def arrived(stage, slot, plane):
        remote(
            win.at[stage, slot, plane], stage, slot, plane, 0, partner[SIB]
        ).wait_recv()

    loads[0].wait()
    for copy in own_sends(0):
        copy.start()

    for load in loads[1:]:
        load.wait()

    def put(slot, real, imag, imag_right):
        for row, value in ((0, real), (M, imag)):
            high, low = split(value)
            left_of[slot, pl.ds(row, M), pl.ds(0, M)] = high
            left_of[slot, pl.ds(row, M), pl.ds(M, M)] = low
            left_of[slot, pl.ds(row, M), pl.ds(2 * M, M)] = high
        for column, value in ((0, real), (M, imag_right)):
            high, low = split(value)
            right_of[slot, pl.ds(0, M), pl.ds(column, M)] = high
            right_of[slot, pl.ds(M, M), pl.ds(column, M)] = low
            right_of[slot, pl.ds(2 * M, M), pl.ds(column, M)] = high

    for k in range(MODES):
        value = raw[k]
        raw[k] = (value + value.T) * 0.5
    for k in range(2):
        value = raw[3 + 2 * k]
        herm[k, 0] = (value + value.T) * 0.5
        value = raw[4 + 2 * k]
        herm[k, 1] = (value - value.T) * 0.5

    rate = jnp.float32(0.0)
    for k in range(MODES):
        rate = rate + occ[0, k].astype(F32) * damp[k]

    for slot in range(4):
        real = jnp.zeros((M, M), F32)
        imag = jnp.zeros((M, M), F32)
        for k in range(MODES):
            raises = jnp.where(up[0, k] == partner[slot], 1.0, 0.0).astype(F32)
            lowers = jnp.where(
                down[0, k] == partner[slot], occ[0, k].astype(F32), 0.0
            ).astype(F32)
            real = real + (raises + lowers * bath[0, k]) * raw[k]
            imag = imag + (lowers * bath[1, k]) * raw[k]
        put(slot, real, imag, imag)

    acc[...] = jnp.zeros_like(acc)

    def add(slot, plane, value):
        high, low = split(value)
        left = jnp.dot(
            left_of[slot],
            jnp.concatenate([high, high, low], axis=0),
            preferred_element_type=F32,
        )
        right = jnp.dot(
            jnp.concatenate([high, high, low], axis=1),
            right_of[slot],
            preferred_element_type=F32,
        )
        minus = left[:M] - right[:, :M]
        plus = left[M:] + right[:, M:]
        if plane == RE:
            return minus, plus
        return -plus, minus

    drive = [np.float32(AMP) * np.cos(np.float32(FREQ * t)) for t in (0.0, STEP / 2, STEP)]

    def stage_body(stage, carry):
        now = jnp.where(
            stage == 0, drive[0], jnp.where(stage == STAGES - 1, drive[2], drive[1])
        ).astype(F32)
        real = herm[0, 0] + now * herm[1, 0]
        imag = herm[0, 1] + now * herm[1, 1]
        put(OWN, real, imag, -imag)

        for plane in (RE, IM):
            first, second = add(OWN, plane, ybuf[stage, plane])
            if plane == RE:
                total[0] = first
                total[1] = second
            else:
                total[0] += first
                total[1] += second

        def take(slot, plane):
            first, second = add(slot, plane, win[stage, slot, plane])
            total[0] += first
            total[1] += second

        hand = forwards(stage)
        arrived(stage, SIB, RE)
        take(SIB, RE)
        arrived(stage, SIB, IM)
        take(SIB, IM)
        arrived(stage, FAR, RE)
        hand[0].start()
        take(FAR, RE)
        arrived(stage, NEAR, IM)
        hand[1].start()
        take(NEAR, IM)
        arrived(stage, BACK, RE)
        take(BACK, RE)
        arrived(stage, NEAR, RE)
        take(NEAR, RE)
        arrived(stage, FAR, IM)
        take(FAR, IM)
        arrived(stage, BACK, IM)
        take(BACK, IM)

        weight = jnp.where((stage == 0) | (stage == STAGES - 1), 1.0, 2.0).astype(F32)
        ahead = jnp.where(stage == 2, STEP, STEP / 2).astype(F32)
        slope_re = total[1] - rate * ybuf[stage, RE]
        slope_im = -total[0] - rate * ybuf[stage, IM]

        @pl.when(stage < STAGES - 1)
        def _():
            ybuf[stage + 1, RE] = ybuf[0, RE] + ahead * slope_re
            ybuf[stage + 1, IM] = ybuf[0, IM] + ahead * slope_im
            for copy in own_sends(stage + 1):
                copy.start()

        acc[RE] += weight * slope_re
        acc[IM] += weight * slope_im
        return carry

    lax.fori_loop(0, STAGES, stage_body, 0)

    out[0] = ybuf[0] + (STEP / 6) * acc[...]

    def drain(stage, carry):
        for copy in own_sends(stage) + forwards(stage):
            copy.wait_send()
        return carry

    lax.fori_loop(0, STAGES, drain, 0)


def on_device(
    state, h_static, drive_op, couple, bath_coef, damping, occupation, raise_nbr, lower_nbr
):
    count = lax.axis_size("aux")
    smem = pl.BlockSpec(memory_space=pltpu.SMEM)
    anywhere = pl.BlockSpec(memory_space=pl.ANY)
    return pl.pallas_call(
        functools.partial(kernel, count),
        out_shape=jax.ShapeDtypeStruct(state.shape, F32),
        in_specs=[smem] * 5 + [anywhere] * 4,
        out_specs=pl.BlockSpec(memory_space=pltpu.VMEM),
        scratch_shapes=[
            pltpu.VMEM((STAGES, 2, M, M), F32),
            pltpu.VMEM((STAGES, 4, 2, M, M), F32),
            pltpu.VMEM((7, M, M), F32),
            pltpu.VMEM((2, 2, M, M), F32),
            pltpu.VMEM((5, 2 * M, 3 * M), BF),
            pltpu.VMEM((5, 3 * M, 2 * M), BF),
            pltpu.VMEM((2, M, M), F32),
            pltpu.VMEM((2, M, M), F32),
            pltpu.SemaphoreType.DMA((4,)),
            pltpu.SemaphoreType.DMA((STAGES, 8)),
            pltpu.SemaphoreType.DMA((STAGES, 4, 2)),
        ],
        compiler_params=pltpu.CompilerParams(
            collective_id=0, has_side_effects=True, vmem_limit_bytes=48 << 20
        ),
        name="rk_step",
    )(
        bath_coef,
        damping,
        occupation,
        raise_nbr,
        lower_nbr,
        state,
        h_static,
        drive_op,
        couple,
    )


def solution(mesh):
    return jax.shard_map(
        on_device,
        mesh=mesh,
        in_specs=(
            P("aux", None, None, None),
            P(),
            P(),
            P(),
            P(),
            P(),
            P("aux", None),
            P("aux", None),
            P("aux", None),
        ),
        out_specs=P("aux", None, None, None),
        check_vma=False,
    )
```

```python
import functools

import jax
import jax.numpy as jnp
import numpy as np
from jax import lax
from jax.experimental import pallas as pl
from jax.experimental.pallas import tpu as pltpu
from jax.sharding import PartitionSpec as P

MESH = pl.DeviceIdType.MESH
STEP = 0.05
AMP = 2.0
FREQ = 20.0
M = 256
HALF = 128
MODES = 3
STAGES = 4
SIB, FAR, NEAR, BACK, OWN = range(5)
RE, IM = 0, 1
BF = jnp.bfloat16
F32 = jnp.float32


def split(value):
    high = value.astype(BF)
    return high, (value - high.astype(F32)).astype(BF)


def kernel(
    count,
    bath_hbm,
    damp_hbm,
    occ_hbm,
    up_hbm,
    down_hbm,
    state,
    h_static,
    drive_op,
    couple,
    out,
    bath,
    damp,
    occ,
    up,
    down,
    ybuf,
    win,
    raw,
    herm,
    left_of,
    right_of,
    total,
    acc,
    load_sem,
    send_sem,
    recv_sem,
):
    me = lax.axis_index("aux")
    odd = lax.rem(me, 2)
    even = odd == 0
    d = 1 - 2 * odd

    def at(offset):
        return lax.rem(me + offset + count, count)

    partner = [at(d), at(2 * d), at(-d), at(-2 * d)]
    chip = me // 2
    last = count // 2 - 1
    has_far = (chip + d >= 0) & (chip + d <= last)
    has_back = (chip - d >= 0) & (chip - d <= last)

    moves = [
        (state.at[0], ybuf.at[0]),
        (h_static, raw.at[pl.ds(3, 2)]),
        (drive_op, raw.at[pl.ds(5, 2)]),
        (couple, raw.at[pl.ds(0, 3)]),
        (bath_hbm, bath),
        (damp_hbm, damp),
        (occ_hbm, occ),
        (up_hbm, up),
        (down_hbm, down),
    ]
    loads = [
        pltpu.make_async_copy(src, dst, load_sem.at[i])
        for i, (src, dst) in enumerate(moves)
    ]
    for load in loads:
        load.start()

    barrier = pltpu.get_barrier_semaphore()

    def greet(slot):
        pl.semaphore_signal(
            barrier, inc=1, device_id=(partner[slot],), device_id_type=MESH
        )

    greet(SIB)

    @pl.when(has_far)
    def _():
        greet(FAR)

    @pl.when(has_back)
    def _():
        greet(NEAR)
        greet(BACK)

    pl.semaphore_wait(
        barrier, 1 + jnp.where(has_far, 1, 0) + jnp.where(has_back, 2, 0)
    )

    def rows(ref, half):
        return ref if half is None else ref.at[pl.ds(half * HALF, HALF)]

    def remote(src, stage, slot, plane, half, number, device):
        part = 0 if half is None else half
        return pltpu.make_async_remote_copy(
            src_ref=rows(src, half),
            dst_ref=rows(win.at[stage, slot, plane], half),
            send_sem=send_sem.at[stage, number, part],
            recv_sem=recv_sem.at[stage, slot, plane, part],
            device_id=(device,),
            device_id_type=MESH,
        )

    def to_back_real(stage):
        return [remote(ybuf.at[stage, RE], stage, FAR, RE, None, 0, partner[BACK])]

    def to_back_imag(stage):
        return [remote(ybuf.at[stage, IM], stage, NEAR, IM, 0, 1, partner[NEAR])]

    def to_back_late(stage):
        return [remote(win.at[stage, SIB, IM], stage, BACK, IM, 1, 1, partner[NEAR])]

    def to_far_real(stage):
        return [remote(ybuf.at[stage, RE], stage, BACK, RE, 0, 2, partner[FAR])]

    def to_far_late(stage):
        return [
            remote(win.at[stage, SIB, IM], stage, NEAR, IM, 1, 3, partner[FAR]),
            remote(ybuf.at[stage, RE], stage, BACK, RE, 1, 2, partner[FAR]),
            remote(ybuf.at[stage, IM], stage, BACK, IM, 0, 3, partner[FAR]),
        ]

    def to_sibling(stage):
        return [
            remote(ybuf.at[stage, IM], stage, SIB, IM, 1, 4, partner[SIB]),
            remote(ybuf.at[stage, IM], stage, SIB, IM, 0, 4, partner[SIB]),
            remote(ybuf.at[stage, RE], stage, SIB, RE, None, 5, partner[SIB]),
        ]

    def hand_real(stage):
        return [remote(win.at[stage, FAR, RE], stage, NEAR, RE, None, 6, partner[SIB])]

    def hand_imag(stage, half):
        return [remote(win.at[stage, NEAR, IM], stage, FAR, IM, half, 7, partner[SIB])]

    def start(copies):
        for copy in copies:
            copy.start()

    def send_real(stage):
        @pl.when(has_back)
        def _():
            start(to_back_real(stage))

        @pl.when(has_far)
        def _():
            start(to_far_real(stage))

    def send_imag(stage):
        @pl.when(has_back)
        def _():
            start(to_back_imag(stage))

        start(to_sibling(stage))

    def arrived(stage, slot, plane, half=None):
        remote(
            win.at[stage, slot, plane], stage, slot, plane, half, 0, partner[SIB]
        ).wait_recv()

    def send_late(stage):
        arrived(stage, SIB, IM, 1)

        @pl.when(has_far)
        def _():
            start(to_far_late(stage))

        @pl.when(has_back)
        def _():
            start(to_back_late(stage))

    loads[0].wait()
    send_real(0)
    send_imag(0)

    def put(slot, real, imag, imag_right):
        for row, value in ((0, real), (M, imag)):
            high, low = split(value)
            left_of[slot, pl.ds(row, M), pl.ds(0, M)] = high
            left_of[slot, pl.ds(row, M), pl.ds(M, M)] = low
            left_of[slot, pl.ds(row, M), pl.ds(2 * M, M)] = high
        for column, value in ((0, real), (M, imag_right)):
            high, low = split(value)
            right_of[slot, pl.ds(0, M), pl.ds(column, M)] = high
            right_of[slot, pl.ds(M, M), pl.ds(column, M)] = low
            right_of[slot, pl.ds(2 * M, M), pl.ds(column, M)] = high

    def products(slot, value, wide, begin=0):
        high, low = split(value)
        size = 2 * M if wide else M
        left = jnp.dot(
            left_of[slot, pl.ds(begin, size)],
            jnp.concatenate([high, high, low], axis=0),
            preferred_element_type=F32,
        )
        right = jnp.dot(
            jnp.concatenate([high, high, low], axis=1),
            right_of[slot, :, pl.ds(begin, size)],
            preferred_element_type=F32,
        )
        return left, right

    def own_products(stage):
        slot = OWN + (stage + 1) // 2
        real, imag = ybuf[stage, RE], ybuf[stage, IM]
        left, right = products(slot, real, True)
        total[0] = rate * imag + (left[:M] - right[:, :M])
        total[1] = (left[M:] + right[:, M:]) - rate * real
        left, right = products(slot, imag, True)
        total[0] -= left[M:] + right[:, M:]
        total[1] += left[:M] - right[:, :M]

    def take_complex(stage, slot, plane):
        left, right = products(slot, win[stage, slot, plane], True)
        minus = left[:M] - right[:, :M]
        plus = left[M:] + right[:, M:]
        if plane == RE:
            total[0] += minus
            total[1] += plus
        else:
            total[0] -= plus
            total[1] += minus

    def take_real(stage, slot, plane):
        left, right = products(slot, win[stage, slot, plane], False)
        total[plane] += left - right

    def take(stage, slot, plane):
        real = even if slot in (SIB, FAR) else jnp.logical_not(even)

        @pl.when(real)
        def _():
            take_real(stage, slot, plane)

        @pl.when(jnp.logical_not(real))
        def _():
            take_complex(stage, slot, plane)

    drive = [
        np.float32(AMP) * np.cos(np.float32(FREQ * t)) for t in (0.0, STEP / 2, STEP)
    ]

    def put_own(i):
        real = herm[0, 0] + drive[i] * herm[1, 0]
        imag = herm[0, 1] + drive[i] * herm[1, 1]
        put(OWN + i, real, imag, -imag)

    for load in loads[4:]:
        load.wait()
    rate = jnp.float32(0.0)
    for k in range(MODES):
        rate = rate + occ[0, k].astype(F32) * damp[k]

    loads[1].wait()
    loads[2].wait()
    for k in range(2):
        value = raw[3 + 2 * k]
        herm[k, 0] = (value + value.T) * 0.5
        value = raw[4 + 2 * k]
        herm[k, 1] = (value - value.T) * 0.5
    put_own(0)
    own_products(0)
    send_late(0)

    loads[3].wait()
    for k in range(MODES):
        value = raw[k]
        raw[k] = (value + value.T) * 0.5

    for slot in range(4):
        real = jnp.zeros((M, M), F32)
        imag = jnp.zeros((M, M), F32)
        for k in range(MODES):
            raises = jnp.where(up[0, k] == partner[slot], 1.0, 0.0).astype(F32)
            lowers = jnp.where(
                down[0, k] == partner[slot], occ[0, k].astype(F32), 0.0
            ).astype(F32)
            real = real + (raises + lowers * bath[0, k]) * raw[k]
            imag = imag + (lowers * bath[1, k]) * raw[k]
        put(slot, real, imag, imag)

    put_own(1)
    put_own(2)
    acc[...] = jnp.zeros_like(acc)

    def stage_body(stage, carry):
        arrived(stage, SIB, IM, 0)
        arrived(stage, SIB, RE)
        take(stage, SIB, RE)
        take(stage, SIB, IM)

        @pl.when(has_far)
        def _():
            arrived(stage, FAR, RE)
            start(hand_real(stage))

        @pl.when(has_back)
        def _():
            arrived(stage, NEAR, IM, 1)
            start(hand_imag(stage, 1))

        @pl.when(has_far)
        def _():
            take(stage, FAR, RE)

        @pl.when(has_back)
        def _():
            arrived(stage, NEAR, IM, 0)
            start(hand_imag(stage, 0))
            arrived(stage, NEAR, RE)
            take(stage, NEAR, RE)
            take(stage, NEAR, IM)
            arrived(stage, BACK, RE, 0)
            arrived(stage, BACK, RE, 1)
            take(stage, BACK, RE)

        @pl.when(has_far)
        def _():
            arrived(stage, FAR, IM, 1)
            arrived(stage, FAR, IM, 0)
            take(stage, FAR, IM)

        @pl.when(has_back)
        def _():
            arrived(stage, BACK, IM, 0)
            arrived(stage, BACK, IM, 1)
            take_real(stage, BACK, IM)

        ahead = jnp.where(stage == 2, STEP, STEP / 2).astype(F32)

        @pl.when(stage < STAGES - 1)
        def _():
            ybuf[stage + 1, RE] = ybuf[0, RE] + ahead * total[1]
            send_real(stage + 1)

        @pl.when(has_back & even)
        def _():
            left, right = products(BACK, win[stage, BACK, IM], False, M)
            total[0] -= left + right

        @pl.when(stage < STAGES - 1)
        def _():
            ybuf[stage + 1, IM] = ybuf[0, IM] - ahead * total[0]
            send_imag(stage + 1)
            weight = jnp.where(stage == 0, 1.0, 2.0).astype(F32)
            acc[RE] += weight * total[1]
            acc[IM] -= weight * total[0]
            own_products(stage + 1)
            send_late(stage + 1)

        return carry

    lax.fori_loop(0, STAGES, stage_body, 0)

    out[0, RE] = ybuf[0, RE] + (STEP / 6) * (acc[RE] + total[1])
    out[0, IM] = ybuf[0, IM] + (STEP / 6) * (acc[IM] - total[0])

    def drain(stage, carry):
        for copy in to_sibling(stage):
            copy.wait_send()

        @pl.when(has_back)
        def _():
            for copy in [
                *to_back_real(stage),
                *to_back_imag(stage),
                *to_back_late(stage),
                *hand_imag(stage, 0),
                *hand_imag(stage, 1),
            ]:
                copy.wait_send()

        @pl.when(has_far)
        def _():
            for copy in [
                *to_far_real(stage),
                *to_far_late(stage),
                *hand_real(stage),
            ]:
                copy.wait_send()

        return carry

    lax.fori_loop(0, STAGES, drain, 0)


def on_device(
    state, h_static, drive_op, couple, bath_coef, damping, occupation, raise_nbr, lower_nbr
):
    count = lax.axis_size("aux")
    return pl.pallas_call(
        functools.partial(kernel, count),
        out_shape=jax.ShapeDtypeStruct(state.shape, F32),
        in_specs=[pl.BlockSpec(memory_space=pltpu.HBM)] * 9,
        out_specs=pl.BlockSpec(memory_space=pltpu.VMEM),
        scratch_shapes=[
            pltpu.SMEM((2, MODES), F32),
            pltpu.SMEM((MODES,), F32),
            pltpu.SMEM((1, MODES), jnp.int32),
            pltpu.SMEM((1, MODES), jnp.int32),
            pltpu.SMEM((1, MODES), jnp.int32),
            pltpu.VMEM((STAGES, 2, M, M), F32),
            pltpu.VMEM((STAGES, 4, 2, M, M), F32),
            pltpu.VMEM((7, M, M), F32),
            pltpu.VMEM((2, 2, M, M), F32),
            pltpu.VMEM((OWN + 3, 2 * M, 3 * M), BF),
            pltpu.VMEM((OWN + 3, 3 * M, 2 * M), BF),
            pltpu.VMEM((2, M, M), F32),
            pltpu.VMEM((2, M, M), F32),
            pltpu.SemaphoreType.DMA((9,)),
            pltpu.SemaphoreType.DMA((STAGES, 8, 2)),
            pltpu.SemaphoreType.DMA((STAGES, 4, 2, 2)),
        ],
        compiler_params=pltpu.CompilerParams(
            collective_id=0, has_side_effects=True, vmem_limit_bytes=48 << 20
        ),
        name="rk_step",
    )(
        *(
            pltpu.with_memory_space_constraint(x, pltpu.HBM)
            for x in (
                bath_coef,
                damping,
                occupation,
                raise_nbr,
                lower_nbr,
                state,
                h_static,
                drive_op,
                couple,
            )
        )
    )


def solution(mesh):
    return jax.shard_map(
        on_device,
        mesh=mesh,
        in_specs=(
            P("aux", None, None, None),
            P(),
            P(),
            P(),
            P(),
            P(),
            P("aux", None),
            P("aux", None),
            P("aux", None),
        ),
        out_specs=P("aux", None, None, None),
        check_vma=False,
    )
```

```python
import functools

import jax
import jax.numpy as jnp
import numpy as np
from jax import lax
from jax.experimental import pallas as pl
from jax.experimental.pallas import tpu as pltpu
from jax.sharding import PartitionSpec as P

MESH = pl.DeviceIdType.MESH
STEP = 0.05
AMP = 2.0
FREQ = 20.0
M = 256
HALF = 128
ROW = 16
MODES = 3
STAGES = 4
SIB, FAR, NEAR, BACK, OWN = range(5)
RE, IM = 0, 1
BF = jnp.bfloat16
F32 = jnp.float32


def split(value):
    high = value.astype(BF)
    return high, (value - high.astype(F32)).astype(BF)


def kernel(
    count,
    bath_hbm,
    damp_hbm,
    occ_hbm,
    up_hbm,
    down_hbm,
    state,
    h_static,
    drive_op,
    couple,
    out,
    bath,
    damp,
    occ,
    up,
    down,
    ybuf,
    win,
    raw,
    herm,
    left_of,
    right_of,
    total,
    acc,
    rim,
    zbuf,
    zsib,
    rim_left,
    rim_right,
    extra,
    load_sem,
    send_sem,
    recv_sem,
    rim_send,
    rim_recv,
    z_send,
    z_recv,
):
    me = lax.axis_index("aux")
    odd = lax.rem(me, 2)
    even = odd == 0
    d = 1 - 2 * odd

    def at(offset):
        return lax.rem(me + offset + count, count)

    partner = [at(d), at(2 * d), at(-d), at(-2 * d)]
    chip = me // 2
    last = count // 2 - 1
    has_far = (chip + d >= 0) & (chip + d <= last)
    has_back = (chip - d >= 0) & (chip - d <= last)

    below = (lax.rem(chip, ROW) == ROW - 1) & (chip < last)
    above = (lax.rem(chip, ROW) == 0) & (chip > 0)
    odd_one = jnp.logical_not(even)

    moves = [
        (state.at[0], ybuf.at[0]),
        (h_static, raw.at[pl.ds(3, 2)]),
        (drive_op, raw.at[pl.ds(5, 2)]),
        (couple, raw.at[pl.ds(0, 3)]),
        (bath_hbm, bath),
        (damp_hbm, damp),
        (occ_hbm, occ),
        (up_hbm, up),
        (down_hbm, down),
    ]
    loads = [
        pltpu.make_async_copy(src, dst, load_sem.at[i])
        for i, (src, dst) in enumerate(moves)
    ]
    for load in loads:
        load.start()

    barrier = pltpu.get_barrier_semaphore()

    def greet(slot):
        pl.semaphore_signal(
            barrier, inc=1, device_id=(partner[slot],), device_id_type=MESH
        )

    greet(SIB)

    @pl.when(has_far)
    def _():
        greet(FAR)

    @pl.when(has_back)
    def _():
        greet(NEAR)
        greet(BACK)

    pl.semaphore_wait(
        barrier, 1 + jnp.where(has_far, 1, 0) + jnp.where(has_back, 2, 0)
    )

    def rows(ref, half):
        return ref if half is None else ref.at[pl.ds(half * HALF, HALF)]

    def remote(src, stage, slot, plane, half, number, device):
        part = 0 if half is None else half
        return pltpu.make_async_remote_copy(
            src_ref=rows(src, half),
            dst_ref=rows(win.at[stage, slot, plane], half),
            send_sem=send_sem.at[stage, number, part],
            recv_sem=recv_sem.at[stage, slot, plane, part],
            device_id=(device,),
            device_id_type=MESH,
        )

    def to_back_real(stage, own):
        return [remote(own.at[RE], stage, FAR, RE, None, 0, partner[BACK])]

    def to_back_imag(stage, own):
        return [remote(own.at[IM], stage, NEAR, IM, 0, 1, partner[NEAR])]

    def to_back_late(stage, other):
        return [halfway(other, stage, BACK, 1, partner[NEAR])]

    def to_far_real(stage, own):
        return [remote(own.at[RE], stage, BACK, RE, 0, 2, partner[FAR])]

    def to_far_late(stage, own, other):
        return [
            halfway(other, stage, NEAR, 3, partner[FAR]),
            remote(own.at[RE], stage, BACK, RE, 1, 2, partner[FAR]),
            remote(own.at[IM], stage, BACK, IM, 0, 3, partner[FAR]),
        ]

    def halfway(other, stage, slot, number, device):
        return pltpu.make_async_remote_copy(
            src_ref=other,
            dst_ref=rows(win.at[stage, slot, IM], 1),
            send_sem=send_sem.at[stage, number, 1],
            recv_sem=recv_sem.at[stage, slot, IM, 1],
            device_id=(device,),
            device_id_type=MESH,
        )

    def to_sibling(stage):
        return [
            remote(ybuf.at[stage, IM], stage, SIB, IM, 1, 4, partner[SIB]),
            remote(ybuf.at[stage, IM], stage, SIB, IM, 0, 4, partner[SIB]),
            remote(ybuf.at[stage, RE], stage, SIB, RE, None, 5, partner[SIB]),
        ]

    def part_to_sibling(stage):
        return pltpu.make_async_remote_copy(
            src_ref=rows(zbuf.at[stage, IM], 1),
            dst_ref=zsib.at[stage],
            send_sem=z_send.at[stage],
            recv_sem=z_recv.at[stage],
            device_id=(partner[SIB],),
            device_id_type=MESH,
        )

    def rim_row(i, slot):
        return pltpu.make_async_remote_copy(
            src_ref=up_hbm,
            dst_ref=rim.at[i],
            send_sem=rim_send.at[0 if slot != BACK else 1],
            recv_sem=rim_recv.at[i],
            device_id=(partner[slot],),
            device_id_type=MESH,
        )

    def hand_real(stage):
        return [remote(win.at[stage, FAR, RE], stage, NEAR, RE, None, 6, partner[SIB])]

    def hand_imag(stage, half):
        return [remote(win.at[stage, NEAR, IM], stage, FAR, IM, half, 7, partner[SIB])]

    def start(copies):
        for copy in copies:
            copy.start()

    def back_real(stage, own):
        @pl.when(has_back)
        def _():
            start(to_back_real(stage, own))

    def far_real(stage, own):
        @pl.when(has_far)
        def _():
            start(to_far_real(stage, own))

    def back_imag(stage, own):
        @pl.when(has_back)
        def _():
            start(to_back_imag(stage, own))

    def arrived(stage, slot, plane, half=None):
        remote(
            win.at[stage, slot, plane], stage, slot, plane, half, 0, partner[SIB]
        ).wait_recv()

    def late_far(stage, own, other):
        @pl.when(has_far)
        def _():
            start(to_far_late(stage, own, other))

    def late_back(stage, other):
        @pl.when(has_back)
        def _():
            start(to_back_late(stage, other))

    def send_late(stage):
        arrived(stage, SIB, IM, 1)
        other = rows(win.at[stage, SIB, IM], 1)
        late_far(stage, ybuf.at[stage], other)
        late_back(stage, other)

    loads[0].wait()
    back_real(0, ybuf.at[0])
    far_real(0, ybuf.at[0])
    back_imag(0, ybuf.at[0])
    start(to_sibling(0))

    @pl.when(below & even)
    def _():
        rim_row(1, FAR).start()

    @pl.when(below & odd_one)
    def _():
        rim_row(0, NEAR).start()
        rim_row(0, BACK).start()

    def put(slot, real, imag, imag_right):
        for row, value in ((0, real), (M, imag)):
            high, low = split(value)
            left_of[slot, pl.ds(row, M), pl.ds(0, M)] = high
            left_of[slot, pl.ds(row, M), pl.ds(M, M)] = low
            left_of[slot, pl.ds(row, M), pl.ds(2 * M, M)] = high
        for column, value in ((0, real), (M, imag_right)):
            high, low = split(value)
            right_of[slot, pl.ds(0, M), pl.ds(column, M)] = high
            right_of[slot, pl.ds(M, M), pl.ds(column, M)] = low
            right_of[slot, pl.ds(2 * M, M), pl.ds(column, M)] = high

    def products(slot, value, wide, begin=0):
        high, low = split(value)
        size = 2 * M if wide else M
        left = jnp.dot(
            left_of[slot, pl.ds(begin, size)],
            jnp.concatenate([high, high, low], axis=0),
            preferred_element_type=F32,
        )
        right = jnp.dot(
            jnp.concatenate([high, high, low], axis=1),
            right_of[slot, :, pl.ds(begin, size)],
            preferred_element_type=F32,
        )
        return left, right

    def own_products(stage):
        slot = OWN + (stage + 1) // 2
        real, imag = ybuf[stage, RE], ybuf[stage, IM]
        left, right = products(slot, real, True)
        total[0] = rate * imag + (left[:M] - right[:, :M])
        total[1] = (left[M:] + right[:, M:]) - rate * real
        left, right = products(slot, imag, True)
        total[0] -= left[M:] + right[:, M:]
        total[1] += left[:M] - right[:, :M]

    def received(stage, slot, plane):
        value = win[stage, slot, plane]
        if slot == SIB:
            return value
        who = odd_one if slot == FAR else even
        before = jnp.where(stage == STAGES - 1, STEP, STEP / 2).astype(F32)
        scale = jnp.where(above & who & (stage > 0), before, 0.0).astype(F32)
        which = 1 if slot == BACK else 0
        other = extra[lax.rem(stage, 2), which, 1 - plane]
        return value + (scale if plane == RE else -scale) * other

    def take_complex(stage, slot, plane):
        left, right = products(slot, received(stage, slot, plane), True)
        minus = left[:M] - right[:, :M]
        plus = left[M:] + right[:, M:]
        if plane == RE:
            total[0] += minus
            total[1] += plus
        else:
            total[0] -= plus
            total[1] += minus

    def take_real(stage, slot, plane):
        left, right = products(slot, received(stage, slot, plane), False)
        total[plane] += left - right

    def contribution(i, value):
        high, low = split(value)
        left = jnp.dot(
            rim_left[i],
            jnp.concatenate([high, high, low], axis=0),
            preferred_element_type=F32,
        )
        right = jnp.dot(
            jnp.concatenate([high, high, low], axis=1),
            rim_right[i],
            preferred_element_type=F32,
        )
        return left - right

    def contribute(stage):
        later = lax.rem(stage + 1, 2)
        for plane in (RE, IM):
            own = ybuf[stage, plane]
            extra[later, 0, plane] = contribution(0, own) + contribution(
                1, win[stage, SIB, plane]
            )

        @pl.when(even)
        def _():
            for plane in (RE, IM):
                extra[later, 1, plane] = contribution(2, ybuf[stage, plane])

    def take(stage, slot, plane):
        real = even if slot in (SIB, FAR) else jnp.logical_not(even)

        @pl.when(real)
        def _():
            take_real(stage, slot, plane)

        @pl.when(jnp.logical_not(real))
        def _():
            take_complex(stage, slot, plane)

    drive = [
        np.float32(AMP) * np.cos(np.float32(FREQ * t)) for t in (0.0, STEP / 2, STEP)
    ]

    def put_own(i):
        real = herm[0, 0] + drive[i] * herm[1, 0]
        imag = herm[0, 1] + drive[i] * herm[1, 1]
        put(OWN + i, real, imag, -imag)

    for load in loads[4:]:
        load.wait()
    rate = jnp.float32(0.0)
    for k in range(MODES):
        rate = rate + occ[0, k].astype(F32) * damp[k]

    loads[1].wait()
    loads[2].wait()
    for k in range(2):
        value = raw[3 + 2 * k]
        herm[k, 0] = (value + value.T) * 0.5
        value = raw[4 + 2 * k]
        herm[k, 1] = (value - value.T) * 0.5
    put_own(0)
    own_products(0)
    send_late(0)

    loads[3].wait()
    for k in range(MODES):
        value = raw[k]
        raw[k] = (value + value.T) * 0.5

    for slot in range(4):
        real = jnp.zeros((M, M), F32)
        imag = jnp.zeros((M, M), F32)
        for k in range(MODES):
            raises = jnp.where(up[0, k] == partner[slot], 1.0, 0.0).astype(F32)
            lowers = jnp.where(
                down[0, k] == partner[slot], occ[0, k].astype(F32), 0.0
            ).astype(F32)
            real = real + (raises + lowers * bath[0, k]) * raw[k]
            imag = imag + (lowers * bath[1, k]) * raw[k]
        put(slot, real, imag, imag)

    put_own(1)
    put_own(2)
    acc[...] = jnp.zeros_like(acc)
    extra[...] = jnp.zeros_like(extra)

    def put_rim(i, row, source):
        real = jnp.zeros((M, M), F32)
        for k in range(MODES):
            real = real + jnp.where(rim[row, 0, k] == source, 1.0, 0.0).astype(F32) * raw[k]
        high, low = split(real)
        for j, part in enumerate((high, low, high)):
            rim_left[i, :, pl.ds(j * M, M)] = part
            rim_right[i, pl.ds(j * M, M), :] = part

    @pl.when(above)
    def _():
        rim_row(0, NEAR).wait_recv()
        put_rim(0, 0, me)
        put_rim(1, 0, partner[SIB])

    @pl.when(above & even)
    def _():
        rim_row(1, NEAR).wait_recv()
        put_rim(2, 1, me)

    def usual(stage, ahead):
        @pl.when(has_far)
        def _():
            arrived(stage, FAR, RE)
            start(hand_real(stage))

        @pl.when(has_back)
        def _():
            arrived(stage, NEAR, IM, 1)
            start(hand_imag(stage, 1))

        @pl.when(has_far)
        def _():
            take(stage, FAR, RE)

        @pl.when(has_back)
        def _():
            arrived(stage, NEAR, IM, 0)
            start(hand_imag(stage, 0))
            arrived(stage, NEAR, RE)
            take(stage, NEAR, RE)
            take(stage, NEAR, IM)
            arrived(stage, BACK, RE, 0)
            arrived(stage, BACK, RE, 1)
            take(stage, BACK, RE)

        @pl.when(has_far)
        def _():
            arrived(stage, FAR, IM, 1)
            arrived(stage, FAR, IM, 0)
            take(stage, FAR, IM)

        @pl.when(has_back)
        def _():
            arrived(stage, BACK, IM, 0)
            arrived(stage, BACK, IM, 1)
            take_real(stage, BACK, IM)

        after = stage + 1

        @pl.when(stage < STAGES - 1)
        def _():
            ybuf[after, RE] = ybuf[0, RE] + ahead * total[1]
            back_real(after, ybuf.at[after])
            far_real(after, ybuf.at[after])

        @pl.when(has_back & even)
        def _():
            value = received(stage, BACK, IM)
            left, right = products(BACK, value, False, M)
            total[0] -= left + right

        @pl.when(stage < STAGES - 1)
        def _():
            ybuf[after, IM] = ybuf[0, IM] - ahead * total[0]
            back_imag(after, ybuf.at[after])
            start(to_sibling(after))

    def keep_part(after, ahead):
        zbuf[after, RE] = ybuf[0, RE] + ahead * total[1]
        zbuf[after, IM] = ybuf[0, IM] - ahead * total[0]

    def below_even(stage, ahead):
        after = stage + 1
        arrived(stage, NEAR, IM, 1)
        start(hand_imag(stage, 1))
        arrived(stage, FAR, RE)
        start(hand_real(stage))
        arrived(stage, NEAR, IM, 0)
        start(hand_imag(stage, 0))
        arrived(stage, NEAR, RE)
        take_complex(stage, NEAR, RE)
        take_complex(stage, NEAR, IM)
        arrived(stage, BACK, RE, 0)
        arrived(stage, BACK, RE, 1)
        take_complex(stage, BACK, RE)
        arrived(stage, BACK, IM, 0)
        arrived(stage, BACK, IM, 1)
        take_complex(stage, BACK, IM)

        @pl.when(stage < STAGES - 1)
        def _():
            keep_part(after, ahead)
            start(to_far_real(after, zbuf.at[after]))
            part_to_sibling(after).start()

        take_real(stage, FAR, RE)
        arrived(stage, FAR, IM, 1)
        arrived(stage, FAR, IM, 0)
        take_real(stage, FAR, IM)

        @pl.when(stage < STAGES - 1)
        def _():
            ybuf[after, RE] = ybuf[0, RE] + ahead * total[1]
            start(to_back_real(after, ybuf.at[after]))
            ybuf[after, IM] = ybuf[0, IM] - ahead * total[0]
            start(to_back_imag(after, ybuf.at[after]))
            start(to_sibling(after))

    def below_odd(stage, ahead):
        after = stage + 1
        arrived(stage, FAR, RE)
        start(hand_real(stage))
        take_complex(stage, FAR, RE)
        arrived(stage, NEAR, IM, 1)
        start(hand_imag(stage, 1))
        arrived(stage, NEAR, IM, 0)
        start(hand_imag(stage, 0))
        arrived(stage, FAR, IM, 1)
        arrived(stage, FAR, IM, 0)
        take_complex(stage, FAR, IM)

        @pl.when(stage < STAGES - 1)
        def _():
            keep_part(after, ahead)
            start(to_back_real(after, zbuf.at[after]))
            start(to_back_imag(after, zbuf.at[after]))
            part_to_sibling(after).start()

        take_real(stage, NEAR, IM)
        arrived(stage, NEAR, RE)
        take_real(stage, NEAR, RE)
        arrived(stage, BACK, RE, 0)
        arrived(stage, BACK, RE, 1)
        take_real(stage, BACK, RE)
        arrived(stage, BACK, IM, 0)
        arrived(stage, BACK, IM, 1)
        take_real(stage, BACK, IM)

        @pl.when(stage < STAGES - 1)
        def _():
            ybuf[after, RE] = ybuf[0, RE] + ahead * total[1]
            start(to_far_real(after, ybuf.at[after]))
            ybuf[after, IM] = ybuf[0, IM] - ahead * total[0]
            start(to_sibling(after))

    def late_below(stage):
        arrived(stage, SIB, IM, 1)
        part_to_sibling(stage).wait_recv()
        other = rows(win.at[stage, SIB, IM], 1)

        @pl.when(even)
        def _():
            start(to_far_late(stage, zbuf.at[stage], zsib.at[stage]))
            start(to_back_late(stage, other))

        @pl.when(odd_one)
        def _():
            start(to_far_late(stage, ybuf.at[stage], other))
            start(to_back_late(stage, zsib.at[stage]))

    def stage_body(stage, carry):
        arrived(stage, SIB, IM, 0)
        arrived(stage, SIB, RE)
        take(stage, SIB, RE)
        take(stage, SIB, IM)

        @pl.when(above & (stage < STAGES - 1))
        def _():
            contribute(stage)

        ahead = jnp.where(stage == 2, STEP, STEP / 2).astype(F32)

        @pl.when(jnp.logical_not(below))
        def _():
            usual(stage, ahead)

        @pl.when(below & even)
        def _():
            below_even(stage, ahead)

        @pl.when(below & odd_one)
        def _():
            below_odd(stage, ahead)

        @pl.when(stage < STAGES - 1)
        def _():
            weight = jnp.where(stage == 0, 1.0, 2.0).astype(F32)
            acc[RE] += weight * total[1]
            acc[IM] -= weight * total[0]
            own_products(stage + 1)

        @pl.when((stage < STAGES - 1) & jnp.logical_not(below))
        def _():
            send_late(stage + 1)

        @pl.when((stage < STAGES - 1) & below)
        def _():
            late_below(stage + 1)

        return carry

    lax.fori_loop(0, STAGES, stage_body, 0)

    out[0, RE] = ybuf[0, RE] + (STEP / 6) * (acc[RE] + total[1])
    out[0, IM] = ybuf[0, IM] + (STEP / 6) * (acc[IM] - total[0])

    def drain(stage, carry):
        for copy in to_sibling(stage):
            copy.wait_send()

        @pl.when(has_back)
        def _():
            for copy in [
                *to_back_real(stage, ybuf.at[stage]),
                *to_back_imag(stage, ybuf.at[stage]),
                *to_back_late(stage, zsib.at[stage]),
                *hand_imag(stage, 0),
                *hand_imag(stage, 1),
            ]:
                copy.wait_send()

        @pl.when(has_far)
        def _():
            for copy in [
                *to_far_real(stage, ybuf.at[stage]),
                *to_far_late(stage, ybuf.at[stage], zsib.at[stage]),
                *hand_real(stage),
            ]:
                copy.wait_send()

        @pl.when(below & (stage > 0))
        def _():
            part_to_sibling(stage).wait_send()

        return carry

    lax.fori_loop(0, STAGES, drain, 0)

    @pl.when(below & even)
    def _():
        rim_row(1, FAR).wait_send()

    @pl.when(below & odd_one)
    def _():
        rim_row(0, NEAR).wait_send()
        rim_row(0, BACK).wait_send()


def on_device(
    state, h_static, drive_op, couple, bath_coef, damping, occupation, raise_nbr, lower_nbr
):
    count = lax.axis_size("aux")
    return pl.pallas_call(
        functools.partial(kernel, count),
        out_shape=jax.ShapeDtypeStruct(state.shape, F32),
        in_specs=[pl.BlockSpec(memory_space=pltpu.HBM)] * 9,
        out_specs=pl.BlockSpec(memory_space=pltpu.VMEM),
        scratch_shapes=[
            pltpu.SMEM((2, MODES), F32),
            pltpu.SMEM((MODES,), F32),
            pltpu.SMEM((1, MODES), jnp.int32),
            pltpu.SMEM((1, MODES), jnp.int32),
            pltpu.SMEM((1, MODES), jnp.int32),
            pltpu.VMEM((STAGES, 2, M, M), F32),
            pltpu.VMEM((STAGES, 4, 2, M, M), F32),
            pltpu.VMEM((7, M, M), F32),
            pltpu.VMEM((2, 2, M, M), F32),
            pltpu.VMEM((OWN + 3, 2 * M, 3 * M), BF),
            pltpu.VMEM((OWN + 3, 3 * M, 2 * M), BF),
            pltpu.VMEM((2, M, M), F32),
            pltpu.VMEM((2, M, M), F32),
            pltpu.SMEM((2, 1, MODES), jnp.int32),
            pltpu.VMEM((STAGES, 2, M, M), F32),
            pltpu.VMEM((STAGES, HALF, M), F32),
            pltpu.VMEM((3, M, 3 * M), BF),
            pltpu.VMEM((3, 3 * M, M), BF),
            pltpu.VMEM((2, 2, 2, M, M), F32),
            pltpu.SemaphoreType.DMA((9,)),
            pltpu.SemaphoreType.DMA((STAGES, 8, 2)),
            pltpu.SemaphoreType.DMA((STAGES, 4, 2, 2)),
            pltpu.SemaphoreType.DMA((2,)),
            pltpu.SemaphoreType.DMA((2,)),
            pltpu.SemaphoreType.DMA((STAGES,)),
            pltpu.SemaphoreType.DMA((STAGES,)),
        ],
        compiler_params=pltpu.CompilerParams(
            collective_id=0, has_side_effects=True, vmem_limit_bytes=48 << 20
        ),
        name="rk_step",
    )(
        *(
            pltpu.with_memory_space_constraint(x, pltpu.HBM)
            for x in (
                bath_coef,
                damping,
                occupation,
                raise_nbr,
                lower_nbr,
                state,
                h_static,
                drive_op,
                couple,
            )
        )
    )


def solution(mesh):
    return jax.shard_map(
        on_device,
        mesh=mesh,
        in_specs=(
            P("aux", None, None, None),
            P(),
            P(),
            P(),
            P(),
            P(),
            P("aux", None),
            P("aux", None),
            P("aux", None),
        ),
        out_specs=P("aux", None, None, None),
        check_vma=False,
    )
```

```python
import functools

import jax
import jax.numpy as jnp
import numpy as np
from jax import lax
from jax.experimental import pallas as pl
from jax.experimental.pallas import tpu as pltpu
from jax.sharding import PartitionSpec as P

MESH = pl.DeviceIdType.MESH
STEP = 0.05
AMP = 2.0
FREQ = 20.0
M = 256
HALF = 128
ROW = 16
MODES = 3
STAGES = 4
SIB, FAR, NEAR, BACK, OWN = range(5)
TO_SIB, TO_BACK, TO_FAR = range(3)
RE, IM = 0, 1
BF = jnp.bfloat16
F32 = jnp.float32


def split(value):
    high = value.astype(BF)
    return high, (value - high.astype(F32)).astype(BF)


def kernel(
    count,
    bath_hbm,
    damp_hbm,
    occ_hbm,
    up_hbm,
    down_hbm,
    state,
    h_static,
    drive_op,
    couple,
    out,
    bath,
    damp,
    occ,
    up,
    down,
    ybuf,
    win,
    raw,
    herm,
    left_of,
    right_of,
    total,
    acc,
    rim,
    zbuf,
    zsib,
    rim_left,
    rim_right,
    extra,
    load_sem,
    send_sem,
    recv_sem,
    rim_send,
    rim_recv,
    z_send,
    z_recv,
):
    me = lax.axis_index("aux")
    odd = lax.rem(me, 2)
    even = odd == 0
    d = 1 - 2 * odd

    def at(offset):
        return lax.rem(me + offset + count, count)

    partner = [at(d), at(2 * d), at(-d), at(-2 * d)]
    chip = me // 2
    last = count // 2 - 1
    has_far = (chip + d >= 0) & (chip + d <= last)
    has_back = (chip - d >= 0) & (chip - d <= last)

    below = (lax.rem(chip, ROW) == ROW - 1) & (chip < last)
    above = (lax.rem(chip, ROW) == 0) & (chip > 0)
    odd_one = jnp.logical_not(even)

    moves = [
        (state.at[0], ybuf.at[0]),
        (h_static, raw.at[pl.ds(3, 2)]),
        (drive_op, raw.at[pl.ds(5, 2)]),
        (couple, raw.at[pl.ds(0, 3)]),
        (bath_hbm, bath),
        (damp_hbm, damp),
        (occ_hbm, occ),
        (up_hbm, up),
        (down_hbm, down),
    ]
    barrier = pltpu.get_barrier_semaphore()

    def greet(slot):
        pl.semaphore_signal(
            barrier, inc=1, device_id=(partner[slot],), device_id_type=MESH
        )

    greet(SIB)

    @pl.when(has_far)
    def _():
        greet(FAR)

    @pl.when(has_back)
    def _():
        greet(NEAR)
        greet(BACK)

    loads = [
        pltpu.make_async_copy(src, dst, load_sem.at[i])
        for i, (src, dst) in enumerate(moves)
    ]
    for load in loads:
        load.start()

    pl.semaphore_wait(
        barrier, 1 + jnp.where(has_far, 1, 0) + jnp.where(has_back, 2, 0)
    )

    def rows(ref, half):
        return ref if half is None else ref.at[pl.ds(half * HALF, HALF)]

    def flag(stage, slot, plane, half):
        number = {
            (SIB, RE): 0,
            (SIB, IM): half or 0,
            (FAR, RE): 2,
            (FAR, IM): 3,
            (NEAR, RE): 4,
            (NEAR, IM): 5 + (half or 0),
            (BACK, RE): 7,
            (BACK, IM): 8,
        }[slot, plane]
        return recv_sem.at[stage, number]

    def remote(src, stage, slot, plane, half, group, device):
        return pltpu.make_async_remote_copy(
            src_ref=rows(src, half),
            dst_ref=rows(win.at[stage, slot, plane], half),
            send_sem=send_sem.at[group],
            recv_sem=flag(stage, slot, plane, half),
            device_id=(device,),
            device_id_type=MESH,
        )

    def to_back_real(stage, own, half):
        return [remote(own.at[RE], stage, FAR, RE, half, TO_BACK, partner[BACK])]

    def to_back_imag(stage, own):
        return [remote(own.at[IM], stage, NEAR, IM, 0, TO_BACK, partner[NEAR])]

    def to_back_late(stage, other):
        return [halfway(other, stage, BACK, TO_BACK, partner[NEAR])]

    def to_far_real(stage, own):
        return [remote(own.at[RE], stage, BACK, RE, 0, TO_FAR, partner[FAR])]

    def to_far_late(stage, own, other):
        return [
            halfway(other, stage, NEAR, TO_FAR, partner[FAR]),
            remote(own.at[RE], stage, BACK, RE, 1, TO_FAR, partner[FAR]),
            remote(own.at[IM], stage, BACK, IM, 0, TO_FAR, partner[FAR]),
        ]

    def halfway(other, stage, slot, group, device):
        return pltpu.make_async_remote_copy(
            src_ref=other,
            dst_ref=rows(win.at[stage, slot, IM], 1),
            send_sem=send_sem.at[group],
            recv_sem=flag(stage, slot, IM, 1),
            device_id=(device,),
            device_id_type=MESH,
        )

    def to_sibling(stage):
        return [
            remote(ybuf.at[stage, IM], stage, SIB, IM, 1, TO_SIB, partner[SIB]),
            remote(ybuf.at[stage, IM], stage, SIB, IM, 0, TO_SIB, partner[SIB]),
            remote(ybuf.at[stage, RE], stage, SIB, RE, None, TO_SIB, partner[SIB]),
        ]

    def part_to_sibling(stage):
        return pltpu.make_async_remote_copy(
            src_ref=rows(zbuf.at[stage, IM], 1),
            dst_ref=zsib.at[stage],
            send_sem=z_send,
            recv_sem=z_recv.at[stage - 1],
            device_id=(partner[SIB],),
            device_id_type=MESH,
        )

    def rim_row(i, slot):
        return pltpu.make_async_remote_copy(
            src_ref=up_hbm,
            dst_ref=rim.at[i],
            send_sem=rim_send.at[0 if slot != BACK else 1],
            recv_sem=rim_recv.at[i],
            device_id=(partner[slot],),
            device_id_type=MESH,
        )

    def hand_real(stage):
        return [remote(win.at[stage, FAR, RE], stage, NEAR, RE, None, TO_FAR, partner[SIB])]

    def hand_imag(stage, half):
        return [remote(win.at[stage, NEAR, IM], stage, FAR, IM, half, TO_BACK, partner[SIB])]

    def start(copies):
        for copy in copies:
            copy.start()

    def back_real(stage, own):
        @pl.when(has_back)
        def _():
            start(to_back_real(stage, own, 0))
            start(to_back_real(stage, own, 1))

    def far_real(stage, own):
        @pl.when(has_far)
        def _():
            start(to_far_real(stage, own))

    def back_imag(stage, own):
        @pl.when(has_back)
        def _():
            start(to_back_imag(stage, own))

    def arrived(stage, slot, plane, half=None):
        remote(
            win.at[stage, slot, plane], stage, slot, plane, half, TO_SIB, partner[SIB]
        ).wait_recv()

    def arrived_rest(stage):
        part = win.at[stage, SIB, :, pl.ds(0, M - HALF // 2)]
        pltpu.make_async_remote_copy(
            src_ref=part,
            dst_ref=part,
            send_sem=send_sem.at[TO_SIB],
            recv_sem=flag(stage, SIB, RE, None),
            device_id=(partner[SIB],),
            device_id_type=MESH,
        ).wait_recv()

    def sent(ref, sem):
        pltpu.make_async_remote_copy(
            src_ref=ref,
            dst_ref=ref,
            send_sem=sem,
            recv_sem=z_recv.at[0],
            device_id=(partner[SIB],),
            device_id_type=MESH,
        ).wait_send()

    def late_far(stage, own, other):
        @pl.when(has_far)
        def _():
            start(to_far_late(stage, own, other))

    def late_back(stage, other):
        @pl.when(has_back)
        def _():
            start(to_back_late(stage, other))

    def send_late(stage):
        arrived(stage, SIB, IM, 1)
        other = rows(win.at[stage, SIB, IM], 1)
        late_far(stage, ybuf.at[stage], other)
        late_back(stage, other)

    loads[0].wait()
    back_real(0, ybuf.at[0])
    far_real(0, ybuf.at[0])
    back_imag(0, ybuf.at[0])
    start(to_sibling(0))

    @pl.when(below & even)
    def _():
        rim_row(1, FAR).start()

    @pl.when(below & odd_one)
    def _():
        rim_row(0, NEAR).start()
        rim_row(0, BACK).start()

    def put(slot, real, imag, imag_right):
        for row, value in ((0, real), (M, imag)):
            high, low = split(value)
            left_of[slot, pl.ds(row, M), pl.ds(0, M)] = high
            left_of[slot, pl.ds(row, M), pl.ds(M, M)] = low
            left_of[slot, pl.ds(row, M), pl.ds(2 * M, M)] = high
        for column, value in ((0, real), (M, imag_right)):
            high, low = split(value)
            right_of[slot, pl.ds(0, M), pl.ds(column, M)] = high
            right_of[slot, pl.ds(M, M), pl.ds(column, M)] = low
            right_of[slot, pl.ds(2 * M, M), pl.ds(column, M)] = high

    def products(slot, value, wide, begin=0):
        high, low = split(value)
        size = 2 * M if wide else M
        left = jnp.dot(
            left_of[slot, pl.ds(begin, size)],
            jnp.concatenate([high, high, low], axis=0),
            preferred_element_type=F32,
        )
        right = jnp.dot(
            jnp.concatenate([high, high, low], axis=1),
            right_of[slot, :, pl.ds(begin, size)],
            preferred_element_type=F32,
        )
        return left, right

    def own_products(stage):
        slot = OWN + (stage + 1) // 2
        real, imag = ybuf[stage, RE], ybuf[stage, IM]
        left, right = products(slot, real, True)
        total[0] = rate * imag + (left[:M] - right[:, :M])
        total[1] = (left[M:] + right[:, M:]) - rate * real
        left, right = products(slot, imag, True)
        total[0] -= left[M:] + right[:, M:]
        total[1] += left[:M] - right[:, :M]

    def received(stage, slot, plane):
        value = win[stage, slot, plane]
        if slot == SIB:
            return value
        who = odd_one if slot == FAR else even
        before = jnp.where(stage == STAGES - 1, STEP, STEP / 2).astype(F32)
        scale = jnp.where(above & who & (stage > 0), before, 0.0).astype(F32)
        which = 1 if slot == BACK else 0
        other = extra[lax.rem(stage, 2), which, 1 - plane]
        return value + (scale if plane == RE else -scale) * other

    def take_complex(stage, slot, plane):
        left, right = products(slot, received(stage, slot, plane), True)
        minus = left[:M] - right[:, :M]
        plus = left[M:] + right[:, M:]
        if plane == RE:
            total[0] += minus
            total[1] += plus
        else:
            total[0] -= plus
            total[1] += minus

    def take_real(stage, slot, plane):
        left, right = products(slot, received(stage, slot, plane), False)
        total[plane] += left - right

    def contribution(i, value):
        high, low = split(value)
        left = jnp.dot(
            rim_left[i],
            jnp.concatenate([high, high, low], axis=0),
            preferred_element_type=F32,
        )
        right = jnp.dot(
            jnp.concatenate([high, high, low], axis=1),
            rim_right[i],
            preferred_element_type=F32,
        )
        return left - right

    def contribute(stage):
        later = lax.rem(stage + 1, 2)
        for plane in (RE, IM):
            own = ybuf[stage, plane]
            extra[later, 0, plane] = contribution(0, own) + contribution(
                1, win[stage, SIB, plane]
            )

        @pl.when(even)
        def _():
            for plane in (RE, IM):
                extra[later, 1, plane] = contribution(2, ybuf[stage, plane])

    def take(stage, slot, plane):
        real = even if slot in (SIB, FAR) else jnp.logical_not(even)

        @pl.when(real)
        def _():
            take_real(stage, slot, plane)

        @pl.when(jnp.logical_not(real))
        def _():
            take_complex(stage, slot, plane)

    drive = [
        np.float32(AMP) * np.cos(np.float32(FREQ * t)) for t in (0.0, STEP / 2, STEP)
    ]

    def put_own(i):
        real = herm[0, 0] + drive[i] * herm[1, 0]
        imag = herm[0, 1] + drive[i] * herm[1, 1]
        put(OWN + i, real, imag, -imag)

    for load in loads[4:]:
        load.wait()
    rate = jnp.float32(0.0)
    for k in range(MODES):
        rate = rate + occ[0, k].astype(F32) * damp[k]

    loads[1].wait()
    loads[2].wait()
    for k in range(2):
        value = raw[3 + 2 * k]
        herm[k, 0] = (value + value.T) * 0.5
        value = raw[4 + 2 * k]
        herm[k, 1] = (value - value.T) * 0.5
    put_own(0)
    own_products(0)
    send_late(0)

    loads[3].wait()
    for k in range(MODES):
        value = raw[k]
        raw[k] = (value + value.T) * 0.5

    for slot in range(4):
        real = jnp.zeros((M, M), F32)
        imag = jnp.zeros((M, M), F32)
        for k in range(MODES):
            raises = jnp.where(up[0, k] == partner[slot], 1.0, 0.0).astype(F32)
            lowers = jnp.where(
                down[0, k] == partner[slot], occ[0, k].astype(F32), 0.0
            ).astype(F32)
            real = real + (raises + lowers * bath[0, k]) * raw[k]
            imag = imag + (lowers * bath[1, k]) * raw[k]
        put(slot, real, imag, imag)

    put_own(1)
    put_own(2)
    acc[...] = jnp.zeros_like(acc)
    extra[...] = jnp.zeros_like(extra)

    def put_rim(i, row, source):
        real = jnp.zeros((M, M), F32)
        for k in range(MODES):
            real = real + jnp.where(rim[row, 0, k] == source, 1.0, 0.0).astype(F32) * raw[k]
        high, low = split(real)
        for j, part in enumerate((high, low, high)):
            rim_left[i, :, pl.ds(j * M, M)] = part
            rim_right[i, pl.ds(j * M, M), :] = part

    @pl.when(above)
    def _():
        rim_row(0, NEAR).wait_recv()
        put_rim(0, 0, me)
        put_rim(1, 0, partner[SIB])

    @pl.when(above & even)
    def _():
        rim_row(1, NEAR).wait_recv()
        put_rim(2, 1, me)

    def usual(stage, ahead):
        @pl.when(has_far)
        def _():
            arrived(stage, FAR, RE)
            start(hand_real(stage))

        @pl.when(has_back)
        def _():
            arrived(stage, NEAR, IM, 1)
            start(hand_imag(stage, 1))

        @pl.when(has_far)
        def _():
            take(stage, FAR, RE)

        @pl.when(has_back)
        def _():
            arrived(stage, NEAR, IM, 0)
            start(hand_imag(stage, 0))
            arrived(stage, NEAR, RE)
            take(stage, NEAR, RE)
            take(stage, NEAR, IM)
            arrived(stage, BACK, RE)
            take(stage, BACK, RE)

        @pl.when(has_far)
        def _():
            arrived(stage, FAR, IM)
            take(stage, FAR, IM)

        after = stage + 1
        more = stage < STAGES - 1

        @pl.when(has_back)
        def _():
            arrived(stage, BACK, IM)

        @pl.when(has_back & more)
        def _():
            high, low = split(received(stage, BACK, IM))
            tall = jnp.concatenate([high, high, low], axis=0)
            for half in (0, 1):
                top = half * HALF
                part = pl.ds(top, HALF)
                left = jnp.dot(
                    left_of[BACK, part], tall, preferred_element_type=F32
                )
                wide = [x[top : top + HALF] for x in (high, high, low)]
                right = jnp.dot(
                    jnp.concatenate(wide, axis=1),
                    right_of[BACK, :, pl.ds(0, M)],
                    preferred_element_type=F32,
                )
                slope = total[1, part] + (left - right)
                total[1, part] = slope
                ybuf[after, RE, part] = ybuf[0, RE, part] + ahead * slope
                start(to_back_real(after, ybuf.at[after], half))
                if half == 0:
                    far_real(after, ybuf.at[after])

        @pl.when(has_back & jnp.logical_not(more))
        def _():
            take_real(stage, BACK, IM)

        @pl.when(jnp.logical_not(has_back) & more)
        def _():
            ybuf[after, RE] = ybuf[0, RE] + ahead * total[1]
            far_real(after, ybuf.at[after])

        @pl.when(has_back & even)
        def _():
            value = received(stage, BACK, IM)
            left, right = products(BACK, value, False, M)
            total[0] -= left + right

        @pl.when(stage < STAGES - 1)
        def _():
            ybuf[after, IM] = ybuf[0, IM] - ahead * total[0]
            back_imag(after, ybuf.at[after])
            start(to_sibling(after))

    def keep_real(after, ahead):
        zbuf[after, RE] = ybuf[0, RE] + ahead * total[1]

    def keep_imag(after, ahead):
        zbuf[after, IM] = ybuf[0, IM] - ahead * total[0]

    def take_rest(stage, slot):
        left, right = products(slot, received(stage, slot, IM), False, M)
        total[0] -= left + right

    def below_even(stage, ahead):
        after = stage + 1
        arrived(stage, NEAR, IM, 1)
        start(hand_imag(stage, 1))
        arrived(stage, FAR, RE)
        start(hand_real(stage))
        arrived(stage, NEAR, IM, 0)
        start(hand_imag(stage, 0))
        arrived(stage, NEAR, RE)
        take_complex(stage, NEAR, RE)
        take_complex(stage, NEAR, IM)
        arrived(stage, BACK, RE)
        take_complex(stage, BACK, RE)
        arrived(stage, BACK, IM)
        take_real(stage, BACK, IM)

        @pl.when(stage < STAGES - 1)
        def _():
            keep_real(after, ahead)
            start(to_far_real(after, zbuf.at[after]))

        take_rest(stage, BACK)

        @pl.when(stage < STAGES - 1)
        def _():
            keep_imag(after, ahead)
            part_to_sibling(after).start()

        take_real(stage, FAR, RE)
        arrived(stage, FAR, IM)
        take_real(stage, FAR, IM)

        @pl.when(stage < STAGES - 1)
        def _():
            ybuf[after, RE] = ybuf[0, RE] + ahead * total[1]
            start(to_back_real(after, ybuf.at[after], 0))
            start(to_back_real(after, ybuf.at[after], 1))
            ybuf[after, IM] = ybuf[0, IM] - ahead * total[0]
            start(to_back_imag(after, ybuf.at[after]))
            start(to_sibling(after))

    def below_odd(stage, ahead):
        after = stage + 1
        arrived(stage, FAR, RE)
        start(hand_real(stage))
        take_complex(stage, FAR, RE)
        arrived(stage, NEAR, IM, 1)
        start(hand_imag(stage, 1))
        arrived(stage, NEAR, IM, 0)
        start(hand_imag(stage, 0))
        arrived(stage, FAR, IM)
        take_real(stage, FAR, IM)

        @pl.when(stage < STAGES - 1)
        def _():
            keep_real(after, ahead)
            start(to_back_real(after, zbuf.at[after], 0))
            start(to_back_real(after, zbuf.at[after], 1))

        take_rest(stage, FAR)

        @pl.when(stage < STAGES - 1)
        def _():
            keep_imag(after, ahead)
            start(to_back_imag(after, zbuf.at[after]))
            part_to_sibling(after).start()

        take_real(stage, NEAR, IM)
        arrived(stage, NEAR, RE)
        take_real(stage, NEAR, RE)
        arrived(stage, BACK, RE)
        take_real(stage, BACK, RE)
        arrived(stage, BACK, IM)
        take_real(stage, BACK, IM)

        @pl.when(stage < STAGES - 1)
        def _():
            ybuf[after, RE] = ybuf[0, RE] + ahead * total[1]
            start(to_far_real(after, ybuf.at[after]))
            ybuf[after, IM] = ybuf[0, IM] - ahead * total[0]
            start(to_sibling(after))

    def late_below(stage):
        arrived(stage, SIB, IM, 1)
        part_to_sibling(stage).wait_recv()
        other = rows(win.at[stage, SIB, IM], 1)

        @pl.when(even)
        def _():
            start(to_far_late(stage, zbuf.at[stage], zsib.at[stage]))
            start(to_back_late(stage, other))

        @pl.when(odd_one)
        def _():
            start(to_far_late(stage, ybuf.at[stage], other))
            start(to_back_late(stage, zsib.at[stage]))

    def stage_body(stage, carry):
        arrived_rest(stage)
        take(stage, SIB, RE)
        take(stage, SIB, IM)

        @pl.when(above & (stage < STAGES - 1))
        def _():
            contribute(stage)

        ahead = jnp.where(stage == 2, STEP, STEP / 2).astype(F32)

        @pl.when(jnp.logical_not(below))
        def _():
            usual(stage, ahead)

        @pl.when(below & even)
        def _():
            below_even(stage, ahead)

        @pl.when(below & odd_one)
        def _():
            below_odd(stage, ahead)

        @pl.when(stage < STAGES - 1)
        def _():
            weight = jnp.where(stage == 0, 1.0, 2.0).astype(F32)
            acc[RE] += weight * total[1]
            acc[IM] -= weight * total[0]
            own_products(stage + 1)

        @pl.when((stage < STAGES - 1) & jnp.logical_not(below))
        def _():
            send_late(stage + 1)

        @pl.when((stage < STAGES - 1) & below)
        def _():
            late_below(stage + 1)

        return carry

    lax.fori_loop(0, STAGES, stage_body, 0)

    out[0, RE] = ybuf[0, RE] + (STEP / 6) * (acc[RE] + total[1])
    out[0, IM] = ybuf[0, IM] + (STEP / 6) * (acc[IM] - total[0])

    sent(ybuf, send_sem.at[TO_SIB])
    most = win.at[pl.ds(0, 2), pl.ds(0, 3)]

    @pl.when(has_back)
    def _():
        sent(most, send_sem.at[TO_BACK])

    @pl.when(has_far)
    def _():
        sent(most, send_sem.at[TO_FAR])

    @pl.when(below)
    def _():
        sent(zsib.at[pl.ds(0, STAGES - 1)], z_send)

    @pl.when(below & even)
    def _():
        rim_row(1, FAR).wait_send()

    @pl.when(below & odd_one)
    def _():
        rim_row(0, NEAR).wait_send()
        rim_row(0, BACK).wait_send()


def on_device(
    state, h_static, drive_op, couple, bath_coef, damping, occupation, raise_nbr, lower_nbr
):
    count = lax.axis_size("aux")
    return pl.pallas_call(
        functools.partial(kernel, count),
        out_shape=jax.ShapeDtypeStruct(state.shape, F32),
        in_specs=[pl.BlockSpec(memory_space=pltpu.HBM)] * 9,
        out_specs=pl.BlockSpec(memory_space=pltpu.VMEM),
        scratch_shapes=[
            pltpu.SMEM((2, MODES), F32),
            pltpu.SMEM((MODES,), F32),
            pltpu.SMEM((1, MODES), jnp.int32),
            pltpu.SMEM((1, MODES), jnp.int32),
            pltpu.SMEM((1, MODES), jnp.int32),
            pltpu.VMEM((STAGES, 2, M, M), F32),
            pltpu.VMEM((STAGES, 4, 2, M, M), F32),
            pltpu.VMEM((7, M, M), F32),
            pltpu.VMEM((2, 2, M, M), F32),
            pltpu.VMEM((OWN + 3, 2 * M, 3 * M), BF),
            pltpu.VMEM((OWN + 3, 3 * M, 2 * M), BF),
            pltpu.VMEM((2, M, M), F32),
            pltpu.VMEM((2, M, M), F32),
            pltpu.SMEM((2, 1, MODES), jnp.int32),
            pltpu.VMEM((STAGES, 2, M, M), F32),
            pltpu.VMEM((STAGES, HALF, M), F32),
            pltpu.VMEM((3, M, 3 * M), BF),
            pltpu.VMEM((3, 3 * M, M), BF),
            pltpu.VMEM((2, 2, 2, M, M), F32),
            pltpu.SemaphoreType.DMA((9,)),
            pltpu.SemaphoreType.DMA((3,)),
            pltpu.SemaphoreType.DMA((STAGES, 9)),
            pltpu.SemaphoreType.DMA((2,)),
            pltpu.SemaphoreType.DMA((2,)),
            pltpu.SemaphoreType.DMA,
            pltpu.SemaphoreType.DMA((STAGES - 1,)),
        ],
        compiler_params=pltpu.CompilerParams(
            collective_id=0, has_side_effects=True, vmem_limit_bytes=48 << 20
        ),
        name="rk_step",
    )(
        *(
            pltpu.with_memory_space_constraint(x, pltpu.HBM)
            for x in (
                bath_coef,
                damping,
                occupation,
                raise_nbr,
                lower_nbr,
                state,
                h_static,
                drive_op,
                couple,
            )
        )
    )


def solution(mesh):
    return jax.shard_map(
        on_device,
        mesh=mesh,
        in_specs=(
            P("aux", None, None, None),
            P(),
            P(),
            P(),
            P(),
            P(),
            P("aux", None),
            P("aux", None),
            P("aux", None),
        ),
        out_specs=P("aux", None, None, None),
        check_vma=False,
    )
```

```python
import functools

import jax
import jax.numpy as jnp
import numpy as np
from jax import lax
from jax.experimental import pallas as pl
from jax.experimental.pallas import tpu as pltpu
from jax.sharding import PartitionSpec as P

MESH = pl.DeviceIdType.MESH
STEP = 0.05
AMP = 2.0
FREQ = 20.0
M = 256
HALF = 128
ROW = 16
MODES = 3
STAGES = 4
SIB, FAR, NEAR, BACK, OWN = range(5)
TO_SIB, TO_BACK, TO_FAR = range(3)
RE, IM = 0, 1
BF = jnp.bfloat16
F32 = jnp.float32


def split(value):
    high = value.astype(BF)
    return high, (value - high.astype(F32)).astype(BF)


def kernel(
    count,
    bath_hbm,
    damp_hbm,
    occ_hbm,
    up_hbm,
    down_hbm,
    state,
    h_static,
    drive_op,
    couple,
    out,
    bath,
    damp,
    occ,
    up,
    down,
    ybuf,
    win,
    raw,
    herm,
    left_of,
    right_of,
    total,
    acc,
    rim,
    zbuf,
    zsib,
    rim_left,
    rim_right,
    extra,
    load_sem,
    send_sem,
    recv_sem,
    rim_send,
    rim_recv,
    z_send,
    z_recv,
):
    me = lax.axis_index("aux")
    odd = lax.rem(me, 2)
    even = odd == 0
    d = 1 - 2 * odd

    def at(offset):
        return lax.rem(me + offset + count, count)

    partner = [at(d), at(2 * d), at(-d), at(-2 * d)]
    chip = me // 2
    last = count // 2 - 1
    has_far = (chip + d >= 0) & (chip + d <= last)
    has_back = (chip - d >= 0) & (chip - d <= last)

    below = (lax.rem(chip, ROW) == ROW - 1) & (chip < last)
    above = (lax.rem(chip, ROW) == 0) & (chip > 0)
    odd_one = jnp.logical_not(even)
    across = (below & odd_one) | (above & even)

    moves = [
        (state.at[0], ybuf.at[0]),
        (h_static, raw.at[pl.ds(3, 2)]),
        (drive_op, raw.at[pl.ds(5, 2)]),
        (couple, raw.at[pl.ds(0, 3)]),
        (bath_hbm, bath),
        (damp_hbm, damp),
        (occ_hbm, occ),
        (up_hbm, up),
        (down_hbm, down),
    ]
    barrier = pltpu.get_barrier_semaphore()

    def greet(slot):
        pl.semaphore_signal(
            barrier, inc=1, device_id=(partner[slot],), device_id_type=MESH
        )

    greet(SIB)

    @pl.when(has_far)
    def _():
        greet(FAR)

    @pl.when(has_back)
    def _():
        greet(BACK)

    @pl.when(across)
    def _():
        greet(NEAR)

    loads = [
        pltpu.make_async_copy(src, dst, load_sem.at[max(i, 3) - 3 if i else 6])
        for i, (src, dst) in enumerate(moves)
    ]
    for load in loads:
        load.start()

    pl.semaphore_wait(
        barrier,
        1
        + jnp.where(has_far, 1, 0)
        + jnp.where(has_back, 1, 0)
        + jnp.where(across, 1, 0),
    )

    def rows(ref, half):
        return ref if half is None else ref.at[pl.ds(half * HALF, HALF)]

    def flag(stage, slot, plane, half):
        number = {
            (SIB, RE): 0,
            (SIB, IM): 1,
            (FAR, RE): 2,
            (FAR, IM): 3,
            (NEAR, RE): 4,
            (NEAR, IM): 5 + (half or 0),
            (BACK, RE): 7,
            (BACK, IM): 8,
        }[slot, plane]
        return recv_sem.at[stage, number]

    def remote(src, stage, slot, plane, half, group, device):
        return pltpu.make_async_remote_copy(
            src_ref=rows(src, half),
            dst_ref=rows(win.at[stage, slot, plane], half),
            send_sem=send_sem.at[group],
            recv_sem=flag(stage, slot, plane, half),
            device_id=(device,),
            device_id_type=MESH,
        )

    def to_back_real(stage, own, half):
        return [remote(own.at[RE], stage, FAR, RE, half, TO_BACK, partner[BACK])]

    def to_far_real(stage, own):
        return [remote(own.at[RE], stage, BACK, RE, 0, TO_FAR, partner[FAR])]

    def to_far_late(stage, own, other):
        return [
            remote(other, stage, NEAR, IM, 1, TO_FAR, partner[FAR]),
            remote(other, stage, NEAR, IM, 0, TO_FAR, partner[FAR]),
            remote(own.at[RE], stage, BACK, RE, 1, TO_FAR, partner[FAR]),
            remote(own.at[IM], stage, BACK, IM, None, TO_FAR, partner[FAR]),
        ]

    def to_sibling(stage):
        return [
            remote(ybuf.at[stage, IM], stage, SIB, IM, None, TO_SIB, partner[SIB]),
            remote(ybuf.at[stage, RE], stage, SIB, RE, None, TO_SIB, partner[SIB]),
        ]

    def part_to_sibling(stage):
        return pltpu.make_async_remote_copy(
            src_ref=zbuf.at[stage, IM],
            dst_ref=zsib.at[stage],
            send_sem=z_send,
            recv_sem=z_recv.at[stage - 1],
            device_id=(partner[SIB],),
            device_id_type=MESH,
        )

    def rim_row(i, slot):
        return pltpu.make_async_remote_copy(
            src_ref=up_hbm,
            dst_ref=rim.at[i],
            send_sem=rim_send.at[0 if slot != BACK else 1],
            recv_sem=rim_recv.at[i],
            device_id=(partner[slot],),
            device_id_type=MESH,
        )

    def hand_real(stage):
        return [remote(win.at[stage, FAR, RE], stage, NEAR, RE, None, TO_FAR, partner[SIB])]

    def hand_imag(stage, half):
        return [remote(win.at[stage, NEAR, IM], stage, FAR, IM, half, TO_BACK, partner[SIB])]

    def start(copies):
        for copy in copies:
            copy.start()

    def back_real(stage, own):
        @pl.when(has_back)
        def _():
            start(to_back_real(stage, own, 0))
            start(to_back_real(stage, own, 1))

    def far_real(stage, own):
        @pl.when(has_far)
        def _():
            start(to_far_real(stage, own))

    def arrived(stage, slot, plane, half=None):
        remote(
            win.at[stage, slot, plane], stage, slot, plane, half, TO_SIB, partner[SIB]
        ).wait_recv()

    def sent(ref, sem):
        pltpu.make_async_remote_copy(
            src_ref=ref,
            dst_ref=ref,
            send_sem=sem,
            recv_sem=z_recv.at[0],
            device_id=(partner[SIB],),
            device_id_type=MESH,
        ).wait_send()

    def late_far(stage, own, other):
        @pl.when(has_far)
        def _():
            start(to_far_late(stage, own, other))

    def send_late(stage):
        arrived(stage, SIB, IM)
        late_far(stage, ybuf.at[stage], win.at[stage, SIB, IM])

    loads[0].wait()
    back_real(0, ybuf.at[0])
    far_real(0, ybuf.at[0])
    start(to_sibling(0))

    @pl.when(below & even)
    def _():
        rim_row(1, FAR).start()

    @pl.when(below & odd_one)
    def _():
        rim_row(0, NEAR).start()
        rim_row(0, BACK).start()

    def put(slot, real, imag, imag_right):
        for row, value in ((0, real), (M, imag)):
            high, low = split(value)
            left_of[slot, pl.ds(row, M), pl.ds(0, M)] = high
            left_of[slot, pl.ds(row, M), pl.ds(M, M)] = low
            left_of[slot, pl.ds(row, M), pl.ds(2 * M, M)] = high
        for column, value in ((0, real), (M, imag_right)):
            high, low = split(value)
            right_of[slot, pl.ds(0, M), pl.ds(column, M)] = high
            right_of[slot, pl.ds(M, M), pl.ds(column, M)] = low
            right_of[slot, pl.ds(2 * M, M), pl.ds(column, M)] = high

    def products(slot, value, wide, begin=0):
        high, low = split(value)
        size = 2 * M if wide else M
        left = jnp.dot(
            left_of[slot, pl.ds(begin, size)],
            jnp.concatenate([high, high, low], axis=0),
            preferred_element_type=F32,
        )
        right = jnp.dot(
            jnp.concatenate([high, high, low], axis=1),
            right_of[slot, :, pl.ds(begin, size)],
            preferred_element_type=F32,
        )
        return left, right

    def own_products(stage, planes):
        slot = OWN + (stage + 1) // 2
        real, imag = ybuf[stage, RE], ybuf[stage, IM]
        if RE in planes:
            left, right = products(slot, real, True)
            total[0] = rate * imag + (left[:M] - right[:, :M])
            total[1] = (left[M:] + right[:, M:]) - rate * real
        if IM in planes:
            left, right = products(slot, imag, True)
            total[0] -= left[M:] + right[:, M:]
            total[1] += left[:M] - right[:, :M]

    def received(stage, slot, plane):
        value = win[stage, slot, plane]
        if slot == SIB:
            return value
        who = odd_one if slot == FAR else even
        before = jnp.where(stage == STAGES - 1, STEP, STEP / 2).astype(F32)
        scale = jnp.where(above & who & (stage > 0), before, 0.0).astype(F32)
        which = 1 if slot == BACK else 0
        other = extra[lax.rem(stage, 2), which, 1 - plane]
        return value + (scale if plane == RE else -scale) * other

    def take_complex(stage, slot, plane):
        left, right = products(slot, received(stage, slot, plane), True)
        minus = left[:M] - right[:, :M]
        plus = left[M:] + right[:, M:]
        if plane == RE:
            total[0] += minus
            total[1] += plus
        else:
            total[0] -= plus
            total[1] += minus

    def take_real(stage, slot, plane):
        left, right = products(slot, received(stage, slot, plane), False)
        total[plane] += left - right

    def contribution(i, value):
        high, low = split(value)
        left = jnp.dot(
            rim_left[i],
            jnp.concatenate([high, high, low], axis=0),
            preferred_element_type=F32,
        )
        right = jnp.dot(
            jnp.concatenate([high, high, low], axis=1),
            rim_right[i],
            preferred_element_type=F32,
        )
        return left - right

    def contribute(stage):
        later = lax.rem(stage + 1, 2)
        for plane in (RE, IM):
            own = ybuf[stage, plane]
            extra[later, 0, plane] = contribution(0, own) + contribution(
                1, win[stage, SIB, plane]
            )

        @pl.when(even)
        def _():
            for plane in (RE, IM):
                extra[later, 1, plane] = contribution(2, ybuf[stage, plane])

    def take(stage, slot, plane):
        real = even if slot in (SIB, FAR) else jnp.logical_not(even)

        @pl.when(real)
        def _():
            take_real(stage, slot, plane)

        @pl.when(jnp.logical_not(real))
        def _():
            take_complex(stage, slot, plane)

    drive = [
        np.float32(AMP) * np.cos(np.float32(FREQ * t)) for t in (0.0, STEP / 2, STEP)
    ]

    def put_own(i):
        real = herm[0, 0] + drive[i] * herm[1, 0]
        imag = herm[0, 1] + drive[i] * herm[1, 1]
        put(OWN + i, real, imag, -imag)

    for load in loads[4:]:
        load.wait()
    rate = jnp.float32(0.0)
    for k in range(MODES):
        rate = rate + occ[0, k].astype(F32) * damp[k]

    pltpu.make_async_copy(raw, raw, load_sem.at[0]).wait()
    for k in range(2):
        value = raw[3 + 2 * k]
        herm[k, 0] = (value + value.T) * 0.5
        value = raw[4 + 2 * k]
        herm[k, 1] = (value - value.T) * 0.5
    put_own(0)
    own_products(0, (RE, IM))
    send_late(0)

    for k in range(MODES):
        value = raw[k]
        raw[k] = (value + value.T) * 0.5

    for slot in range(4):
        real = jnp.zeros((M, M), F32)
        imag = jnp.zeros((M, M), F32)
        for k in range(MODES):
            raises = jnp.where(up[0, k] == partner[slot], 1.0, 0.0).astype(F32)
            lowers = jnp.where(
                down[0, k] == partner[slot], occ[0, k].astype(F32), 0.0
            ).astype(F32)
            real = real + (raises + lowers * bath[0, k]) * raw[k]
            imag = imag + (lowers * bath[1, k]) * raw[k]
        put(slot, real, imag, imag)

    put_own(1)
    put_own(2)
    acc[...] = jnp.zeros_like(acc)
    extra[...] = jnp.zeros_like(extra)

    def put_rim(i, row, source):
        real = jnp.zeros((M, M), F32)
        for k in range(MODES):
            real = real + jnp.where(rim[row, 0, k] == source, 1.0, 0.0).astype(F32) * raw[k]
        high, low = split(real)
        for j, part in enumerate((high, low, high)):
            rim_left[i, :, pl.ds(j * M, M)] = part
            rim_right[i, pl.ds(j * M, M), :] = part

    @pl.when(above)
    def _():
        rim_row(0, NEAR).wait_recv()
        put_rim(0, 0, me)
        put_rim(1, 0, partner[SIB])

    @pl.when(above & even)
    def _():
        rim_row(1, NEAR).wait_recv()
        put_rim(2, 1, me)

    def usual(stage, ahead):
        @pl.when(has_far)
        def _():
            arrived(stage, FAR, RE)
            start(hand_real(stage))

        @pl.when(has_back)
        def _():
            arrived(stage, NEAR, IM, 1)
            start(hand_imag(stage, 1))

        @pl.when(has_far)
        def _():
            take(stage, FAR, RE)

        @pl.when(has_back)
        def _():
            arrived(stage, NEAR, IM, 0)
            start(hand_imag(stage, 0))
            arrived(stage, NEAR, RE)
            take(stage, NEAR, RE)
            take(stage, NEAR, IM)
            arrived(stage, BACK, RE)
            take(stage, BACK, RE)

        @pl.when(has_far)
        def _():
            arrived(stage, FAR, IM)
            take_real(stage, FAR, IM)

        after = stage + 1
        more = stage < STAGES - 1

        @pl.when(has_back)
        def _():
            arrived(stage, BACK, IM)

        @pl.when(has_back & more)
        def _():
            high, low = split(received(stage, BACK, IM))
            tall = jnp.concatenate([high, high, low], axis=0)
            for half in (0, 1):
                top = half * HALF
                part = pl.ds(top, HALF)
                left = jnp.dot(
                    left_of[BACK, part], tall, preferred_element_type=F32
                )
                wide = [x[top : top + HALF] for x in (high, high, low)]
                right = jnp.dot(
                    jnp.concatenate(wide, axis=1),
                    right_of[BACK, :, pl.ds(0, M)],
                    preferred_element_type=F32,
                )
                slope = total[1, part] + (left - right)
                total[1, part] = slope
                ybuf[after, RE, part] = ybuf[0, RE, part] + ahead * slope
                start(to_back_real(after, ybuf.at[after], half))
                if half == 0:
                    far_real(after, ybuf.at[after])

        @pl.when(has_back & jnp.logical_not(more))
        def _():
            take_real(stage, BACK, IM)

        @pl.when(jnp.logical_not(has_back) & more)
        def _():
            ybuf[after, RE] = ybuf[0, RE] + ahead * total[1]
            far_real(after, ybuf.at[after])

        @pl.when(has_back & even)
        def _():
            take_rest(stage, BACK)

        @pl.when(has_far & odd_one)
        def _():
            take_rest(stage, FAR)

        @pl.when(stage < STAGES - 1)
        def _():
            ybuf[after, IM] = ybuf[0, IM] - ahead * total[0]
            start(to_sibling(after))

    def keep_real(after, ahead):
        zbuf[after, RE] = ybuf[0, RE] + ahead * total[1]

    def keep_imag(after, ahead):
        zbuf[after, IM] = ybuf[0, IM] - ahead * total[0]

    def take_rest(stage, slot):
        left, right = products(slot, received(stage, slot, IM), False, M)
        total[0] -= left + right

    def below_even(stage, ahead):
        after = stage + 1
        arrived(stage, NEAR, IM, 1)
        start(hand_imag(stage, 1))
        arrived(stage, FAR, RE)
        start(hand_real(stage))
        arrived(stage, NEAR, IM, 0)
        start(hand_imag(stage, 0))
        arrived(stage, NEAR, RE)
        take_complex(stage, NEAR, RE)
        take_complex(stage, NEAR, IM)
        arrived(stage, BACK, RE)
        take_complex(stage, BACK, RE)
        arrived(stage, BACK, IM)
        take_real(stage, BACK, IM)

        @pl.when(stage < STAGES - 1)
        def _():
            keep_real(after, ahead)
            start(to_far_real(after, zbuf.at[after]))

        take_rest(stage, BACK)

        @pl.when(stage < STAGES - 1)
        def _():
            keep_imag(after, ahead)

        take_real(stage, FAR, RE)
        arrived(stage, FAR, IM)
        take_real(stage, FAR, IM)

        @pl.when(stage < STAGES - 1)
        def _():
            ybuf[after, RE] = ybuf[0, RE] + ahead * total[1]
            start(to_back_real(after, ybuf.at[after], 0))
            start(to_back_real(after, ybuf.at[after], 1))
            ybuf[after, IM] = ybuf[0, IM] - ahead * total[0]
            start(to_sibling(after))

    def below_odd(stage, ahead):
        after = stage + 1
        arrived(stage, FAR, RE)
        start(hand_real(stage))
        take_complex(stage, FAR, RE)
        arrived(stage, NEAR, IM, 1)
        start(hand_imag(stage, 1))
        arrived(stage, NEAR, IM, 0)
        start(hand_imag(stage, 0))
        arrived(stage, FAR, IM)
        take_real(stage, FAR, IM)

        @pl.when(stage < STAGES - 1)
        def _():
            keep_real(after, ahead)
            start(to_back_real(after, zbuf.at[after], 0))
            start(to_back_real(after, zbuf.at[after], 1))

        take_rest(stage, FAR)

        @pl.when(stage < STAGES - 1)
        def _():
            keep_imag(after, ahead)
            part_to_sibling(after).start()

        take_real(stage, NEAR, IM)
        arrived(stage, NEAR, RE)
        take_real(stage, NEAR, RE)
        arrived(stage, BACK, RE)
        take_real(stage, BACK, RE)
        arrived(stage, BACK, IM)
        take_real(stage, BACK, IM)

        @pl.when(stage < STAGES - 1)
        def _():
            ybuf[after, RE] = ybuf[0, RE] + ahead * total[1]
            start(to_far_real(after, ybuf.at[after]))
            ybuf[after, IM] = ybuf[0, IM] - ahead * total[0]
            start(to_sibling(after))

    def late_below(stage):
        @pl.when(even)
        def _():
            part_to_sibling(stage).wait_recv()
            start(to_far_late(stage, zbuf.at[stage], zsib.at[stage]))
            arrived(stage, SIB, IM)

        @pl.when(odd_one)
        def _():
            arrived(stage, SIB, IM)
            start(to_far_late(stage, ybuf.at[stage], win.at[stage, SIB, IM]))

    def stage_body(stage, carry):
        arrived(stage, SIB, RE)
        take(stage, SIB, RE)
        take(stage, SIB, IM)

        @pl.when(above & (stage < STAGES - 1))
        def _():
            contribute(stage)

        ahead = jnp.where(stage == 2, STEP, STEP / 2).astype(F32)

        @pl.when(jnp.logical_not(below))
        def _():
            usual(stage, ahead)

        @pl.when(below & even)
        def _():
            below_even(stage, ahead)

        @pl.when(below & odd_one)
        def _():
            below_odd(stage, ahead)

        @pl.when(stage < STAGES - 1)
        def _():
            weight = jnp.where(stage == 0, 1.0, 2.0).astype(F32)
            acc[RE] += weight * total[1]
            acc[IM] -= weight * total[0]
            own_products(stage + 1, (RE,))

        @pl.when((stage < STAGES - 1) & jnp.logical_not(below))
        def _():
            send_late(stage + 1)

        @pl.when((stage < STAGES - 1) & below)
        def _():
            late_below(stage + 1)

        @pl.when(stage < STAGES - 1)
        def _():
            own_products(stage + 1, (IM,))

        return carry

    lax.fori_loop(0, STAGES, stage_body, 0)

    out[0, RE] = ybuf[0, RE] + (STEP / 6) * (acc[RE] + total[1])
    out[0, IM] = ybuf[0, IM] + (STEP / 6) * (acc[IM] - total[0])

    sent(ybuf, send_sem.at[TO_SIB])

    @pl.when(has_back)
    def _():
        sent(ybuf, send_sem.at[TO_BACK])

    @pl.when(has_far)
    def _():
        sent(win.at[pl.ds(0, 2)], send_sem.at[TO_FAR])

    @pl.when(below & odd_one)
    def _():
        sent(zsib.at[pl.ds(0, STAGES - 1)], z_send)

    @pl.when(below & even)
    def _():
        rim_row(1, FAR).wait_send()

    @pl.when(below & odd_one)
    def _():
        rim_row(0, NEAR).wait_send()
        rim_row(0, BACK).wait_send()


def on_device(
    state, h_static, drive_op, couple, bath_coef, damping, occupation, raise_nbr, lower_nbr
):
    count = lax.axis_size("aux")
    return pl.pallas_call(
        functools.partial(kernel, count),
        out_shape=jax.ShapeDtypeStruct(state.shape, F32),
        in_specs=[pl.BlockSpec(memory_space=pltpu.HBM)] * 9,
        out_specs=pl.BlockSpec(memory_space=pltpu.VMEM),
        scratch_shapes=[
            pltpu.SMEM((2, MODES), F32),
            pltpu.SMEM((MODES,), F32),
            pltpu.SMEM((1, MODES), jnp.int32),
            pltpu.SMEM((1, MODES), jnp.int32),
            pltpu.SMEM((1, MODES), jnp.int32),
            pltpu.VMEM((STAGES, 2, M, M), F32),
            pltpu.VMEM((STAGES, 4, 2, M, M), F32),
            pltpu.VMEM((7, M, M), F32),
            pltpu.VMEM((2, 2, M, M), F32),
            pltpu.VMEM((OWN + 3, 2 * M, 3 * M), BF),
            pltpu.VMEM((OWN + 3, 3 * M, 2 * M), BF),
            pltpu.VMEM((2, M, M), F32),
            pltpu.VMEM((2, M, M), F32),
            pltpu.SMEM((2, 1, MODES), jnp.int32),
            pltpu.VMEM((STAGES, 2, M, M), F32),
            pltpu.VMEM((STAGES, M, M), F32),
            pltpu.VMEM((3, M, 3 * M), BF),
            pltpu.VMEM((3, 3 * M, M), BF),
            pltpu.VMEM((2, 2, 2, M, M), F32),
            pltpu.SemaphoreType.DMA((7,)),
            pltpu.SemaphoreType.DMA((3,)),
            pltpu.SemaphoreType.DMA((STAGES, 9)),
            pltpu.SemaphoreType.DMA((2,)),
            pltpu.SemaphoreType.DMA((2,)),
            pltpu.SemaphoreType.DMA,
            pltpu.SemaphoreType.DMA((STAGES - 1,)),
        ],
        compiler_params=pltpu.CompilerParams(
            collective_id=0, has_side_effects=True, vmem_limit_bytes=48 << 20
        ),
        name="rk_step",
    )(
        *(
            pltpu.with_memory_space_constraint(x, pltpu.HBM)
            for x in (
                bath_coef,
                damping,
                occupation,
                raise_nbr,
                lower_nbr,
                state,
                h_static,
                drive_op,
                couple,
            )
        )
    )


def solution(mesh):
    return jax.shard_map(
        on_device,
        mesh=mesh,
        in_specs=(
            P("aux", None, None, None),
            P(),
            P(),
            P(),
            P(),
            P(),
            P("aux", None),
            P("aux", None),
            P("aux", None),
        ),
        out_specs=P("aux", None, None, None),
        check_vma=False,
    )
```

```python
import functools

import jax
import jax.numpy as jnp
import numpy as np
from jax import lax
from jax.experimental import pallas as pl
from jax.experimental.pallas import tpu as pltpu
from jax.sharding import PartitionSpec as P

MESH = pl.DeviceIdType.MESH
STEP = 0.05
AMP = 2.0
FREQ = 20.0
M = 256
HALF = 128
ROW = 16
MODES = 3
STAGES = 4
SIB, FAR, NEAR, BACK, OWN = range(5)
TO_SIB, TO_BACK, TO_FAR = range(3)
RE, IM = 0, 1
BF = jnp.bfloat16
F32 = jnp.float32


def split(value):
    high = value.astype(BF)
    return high, (value - high.astype(F32)).astype(BF)


def kernel(
    count,
    bath_hbm,
    damp_hbm,
    occ_hbm,
    up_hbm,
    down_hbm,
    state,
    h_static,
    drive_op,
    couple,
    out,
    bath,
    damp,
    occ,
    up,
    down,
    ybuf,
    win,
    raw,
    herm,
    left_of,
    right_of,
    total,
    acc,
    rim,
    zbuf,
    zsib,
    rim_left,
    rim_right,
    extra,
    load_sem,
    send_sem,
    recv_sem,
    rim_send,
    rim_recv,
    z_send,
    z_recv,
):
    me = lax.axis_index("aux")
    odd = lax.rem(me, 2)
    even = odd == 0
    d = 1 - 2 * odd

    def at(offset):
        return lax.rem(me + offset + count, count)

    partner = [at(d), at(2 * d), at(-d), at(-2 * d)]
    chip = me // 2
    last = count // 2 - 1
    has_far = (chip + d >= 0) & (chip + d <= last)
    has_back = (chip - d >= 0) & (chip - d <= last)

    below = (lax.rem(chip, ROW) == ROW - 1) & (chip < last)
    above = (lax.rem(chip, ROW) == 0) & (chip > 0)
    odd_one = jnp.logical_not(even)
    across = (below & odd_one) | (above & even)

    moves = [
        (state.at[0], ybuf.at[0]),
        (h_static, raw.at[pl.ds(3, 2)]),
        (drive_op, raw.at[pl.ds(5, 2)]),
        (couple, raw.at[pl.ds(0, 3)]),
        (bath_hbm, bath),
        (damp_hbm, damp),
        (occ_hbm, occ),
        (up_hbm, up),
        (down_hbm, down),
    ]
    barrier = pltpu.get_barrier_semaphore()

    def greet(slot):
        pl.semaphore_signal(
            barrier, inc=1, device_id=(partner[slot],), device_id_type=MESH
        )

    greet(SIB)

    @pl.when(has_far)
    def _():
        greet(FAR)

    @pl.when(has_back)
    def _():
        greet(BACK)

    @pl.when(across)
    def _():
        greet(NEAR)

    loads = [
        pltpu.make_async_copy(src, dst, load_sem.at[max(i, 3) - 3 if i else 6])
        for i, (src, dst) in enumerate(moves)
    ]
    for load in loads:
        load.start()

    pl.semaphore_wait(
        barrier,
        1
        + jnp.where(has_far, 1, 0)
        + jnp.where(has_back, 1, 0)
        + jnp.where(across, 1, 0),
    )

    def rows(ref, half):
        return ref if half is None else ref.at[pl.ds(half * HALF, HALF)]

    def flag(stage, slot, plane, half):
        number = {
            (SIB, RE): 0,
            (SIB, IM): 1,
            (FAR, RE): 2,
            (FAR, IM): 3,
            (NEAR, RE): 4,
            (NEAR, IM): 5 + (half or 0),
            (BACK, RE): 7,
            (BACK, IM): 8 + (half or 0),
        }[slot, plane]
        return recv_sem.at[stage, number]

    def remote(src, stage, slot, plane, half, group, device):
        return pltpu.make_async_remote_copy(
            src_ref=rows(src, half),
            dst_ref=rows(win.at[stage, slot, plane], half),
            send_sem=send_sem.at[group],
            recv_sem=flag(stage, slot, plane, half),
            device_id=(device,),
            device_id_type=MESH,
        )

    def to_back_real(stage, own, half):
        return [remote(own.at[RE], stage, FAR, RE, half, TO_BACK, partner[BACK])]

    def to_far_real(stage, own):
        return [remote(own.at[RE], stage, BACK, RE, 0, TO_FAR, partner[FAR])]

    def to_far_late(stage, own, other):
        return [
            remote(other, stage, NEAR, IM, 1, TO_FAR, partner[FAR]),
            remote(other, stage, NEAR, IM, 0, TO_FAR, partner[FAR]),
            remote(own.at[RE], stage, BACK, RE, 1, TO_FAR, partner[FAR]),
            remote(own.at[IM], stage, BACK, IM, 0, TO_FAR, partner[FAR]),
            remote(own.at[IM], stage, BACK, IM, 1, TO_FAR, partner[FAR]),
        ]

    def to_sibling(stage):
        return [
            remote(ybuf.at[stage, IM], stage, SIB, IM, None, TO_SIB, partner[SIB]),
            remote(ybuf.at[stage, RE], stage, SIB, RE, None, TO_SIB, partner[SIB]),
        ]

    def part_to_sibling(stage):
        return pltpu.make_async_remote_copy(
            src_ref=zbuf.at[stage, IM],
            dst_ref=zsib.at[stage],
            send_sem=z_send,
            recv_sem=z_recv.at[stage - 1],
            device_id=(partner[SIB],),
            device_id_type=MESH,
        )

    def rim_row(i, slot):
        return pltpu.make_async_remote_copy(
            src_ref=up_hbm,
            dst_ref=rim.at[i],
            send_sem=rim_send.at[0 if slot != BACK else 1],
            recv_sem=rim_recv.at[i],
            device_id=(partner[slot],),
            device_id_type=MESH,
        )

    def hand_real(stage):
        return [remote(win.at[stage, FAR, RE], stage, NEAR, RE, None, TO_FAR, partner[SIB])]

    def hand_imag(stage, half):
        return [remote(win.at[stage, NEAR, IM], stage, FAR, IM, half, TO_BACK, partner[SIB])]

    def start(copies):
        for copy in copies:
            copy.start()

    def back_real(stage, own):
        @pl.when(has_back)
        def _():
            start(to_back_real(stage, own, 0))
            start(to_back_real(stage, own, 1))

    def far_real(stage, own):
        @pl.when(has_far)
        def _():
            start(to_far_real(stage, own))

    def arrived(stage, slot, plane, half=None):
        remote(
            win.at[stage, slot, plane], stage, slot, plane, half, TO_SIB, partner[SIB]
        ).wait_recv()

    def sent(ref, sem):
        pltpu.make_async_remote_copy(
            src_ref=ref,
            dst_ref=ref,
            send_sem=sem,
            recv_sem=z_recv.at[0],
            device_id=(partner[SIB],),
            device_id_type=MESH,
        ).wait_send()

    def late_far(stage, own, other):
        @pl.when(has_far)
        def _():
            start(to_far_late(stage, own, other))

    def send_late(stage):
        arrived(stage, SIB, IM)
        late_far(stage, ybuf.at[stage], win.at[stage, SIB, IM])

    loads[0].wait()
    back_real(0, ybuf.at[0])
    far_real(0, ybuf.at[0])
    start(to_sibling(0))

    @pl.when(below & even)
    def _():
        rim_row(1, FAR).start()

    @pl.when(below & odd_one)
    def _():
        rim_row(0, NEAR).start()
        rim_row(0, BACK).start()

    def put(slot, real, imag, imag_right):
        for row, value in ((0, real), (M, imag)):
            high, low = split(value)
            left_of[slot, pl.ds(row, M), pl.ds(0, M)] = high
            left_of[slot, pl.ds(row, M), pl.ds(M, M)] = low
            left_of[slot, pl.ds(row, M), pl.ds(2 * M, M)] = high
        for column, value in ((0, real), (M, imag_right)):
            high, low = split(value)
            right_of[slot, pl.ds(0, M), pl.ds(column, M)] = high
            right_of[slot, pl.ds(M, M), pl.ds(column, M)] = low
            right_of[slot, pl.ds(2 * M, M), pl.ds(column, M)] = high

    def products(slot, value, wide, begin=0):
        high, low = split(value)
        size = 2 * M if wide else M
        left = jnp.dot(
            left_of[slot, pl.ds(begin, size)],
            jnp.concatenate([high, high, low], axis=0),
            preferred_element_type=F32,
        )
        right = jnp.dot(
            jnp.concatenate([high, high, low], axis=1),
            right_of[slot, :, pl.ds(begin, size)],
            preferred_element_type=F32,
        )
        return left, right

    def own_products(stage, planes):
        slot = OWN + (stage + 1) // 2
        real, imag = ybuf[stage, RE], ybuf[stage, IM]
        if RE in planes:
            left, right = products(slot, real, True)
            total[0] = rate * imag + (left[:M] - right[:, :M])
            total[1] = (left[M:] + right[:, M:]) - rate * real
        if IM in planes:
            left, right = products(slot, imag, True)
            total[0] -= left[M:] + right[:, M:]
            total[1] += left[:M] - right[:, :M]

    def received(stage, slot, plane, part=pl.ds(0, M)):
        value = win[stage, slot, plane, part]
        if slot == SIB:
            return value
        who = odd_one if slot == FAR else even
        before = jnp.where(stage == STAGES - 1, STEP, STEP / 2).astype(F32)
        scale = jnp.where(above & who & (stage > 0), before, 0.0).astype(F32)
        which = 1 if slot == BACK else 0
        other = extra[lax.rem(stage, 2), which, 1 - plane, part]
        return value + (scale if plane == RE else -scale) * other

    def take_complex(stage, slot, plane):
        left, right = products(slot, received(stage, slot, plane), True)
        minus = left[:M] - right[:, :M]
        plus = left[M:] + right[:, M:]
        if plane == RE:
            total[0] += minus
            total[1] += plus
        else:
            total[0] -= plus
            total[1] += minus

    def take_real(stage, slot, plane):
        left, right = products(slot, received(stage, slot, plane), False)
        total[plane] += left - right

    def contribution(i, value):
        high, low = split(value)
        left = jnp.dot(
            rim_left[i],
            jnp.concatenate([high, high, low], axis=0),
            preferred_element_type=F32,
        )
        right = jnp.dot(
            jnp.concatenate([high, high, low], axis=1),
            rim_right[i],
            preferred_element_type=F32,
        )
        return left - right

    def contribute(stage):
        later = lax.rem(stage + 1, 2)
        for plane in (RE, IM):
            own = ybuf[stage, plane]
            extra[later, 0, plane] = contribution(0, own) + contribution(
                1, win[stage, SIB, plane]
            )

        @pl.when(even)
        def _():
            for plane in (RE, IM):
                extra[later, 1, plane] = contribution(2, ybuf[stage, plane])

    def take(stage, slot, plane):
        real = even if slot in (SIB, FAR) else jnp.logical_not(even)

        @pl.when(real)
        def _():
            take_real(stage, slot, plane)

        @pl.when(jnp.logical_not(real))
        def _():
            take_complex(stage, slot, plane)

    drive = [
        np.float32(AMP) * np.cos(np.float32(FREQ * t)) for t in (0.0, STEP / 2, STEP)
    ]

    def put_own(i):
        real = herm[0, 0] + drive[i] * herm[1, 0]
        imag = herm[0, 1] + drive[i] * herm[1, 1]
        put(OWN + i, real, imag, -imag)

    for load in loads[4:]:
        load.wait()
    rate = jnp.float32(0.0)
    for k in range(MODES):
        rate = rate + occ[0, k].astype(F32) * damp[k]

    pltpu.make_async_copy(raw, raw, load_sem.at[0]).wait()
    for k in range(2):
        value = raw[3 + 2 * k]
        herm[k, 0] = (value + value.T) * 0.5
        value = raw[4 + 2 * k]
        herm[k, 1] = (value - value.T) * 0.5
    put_own(0)
    own_products(0, (RE, IM))
    send_late(0)

    for k in range(MODES):
        value = raw[k]
        raw[k] = (value + value.T) * 0.5

    for slot in range(4):
        real = jnp.zeros((M, M), F32)
        imag = jnp.zeros((M, M), F32)
        for k in range(MODES):
            raises = jnp.where(up[0, k] == partner[slot], 1.0, 0.0).astype(F32)
            lowers = jnp.where(
                down[0, k] == partner[slot], occ[0, k].astype(F32), 0.0
            ).astype(F32)
            real = real + (raises + lowers * bath[0, k]) * raw[k]
            imag = imag + (lowers * bath[1, k]) * raw[k]
        put(slot, real, imag, imag)

    put_own(1)
    put_own(2)
    acc[...] = jnp.zeros_like(acc)
    extra[...] = jnp.zeros_like(extra)

    def put_rim(i, row, source):
        real = jnp.zeros((M, M), F32)
        for k in range(MODES):
            real = real + jnp.where(rim[row, 0, k] == source, 1.0, 0.0).astype(F32) * raw[k]
        high, low = split(real)
        for j, part in enumerate((high, low, high)):
            rim_left[i, :, pl.ds(j * M, M)] = part
            rim_right[i, pl.ds(j * M, M), :] = part

    @pl.when(above)
    def _():
        rim_row(0, NEAR).wait_recv()
        put_rim(0, 0, me)
        put_rim(1, 0, partner[SIB])

    @pl.when(above & even)
    def _():
        rim_row(1, NEAR).wait_recv()
        put_rim(2, 1, me)

    def usual(stage, ahead):
        @pl.when(has_far)
        def _():
            arrived(stage, FAR, RE)
            start(hand_real(stage))

        @pl.when(has_back)
        def _():
            arrived(stage, NEAR, IM, 1)
            start(hand_imag(stage, 1))

        @pl.when(has_far)
        def _():
            take(stage, FAR, RE)

        @pl.when(has_back)
        def _():
            arrived(stage, NEAR, IM, 0)
            start(hand_imag(stage, 0))
            arrived(stage, NEAR, RE)
            take(stage, NEAR, RE)
            take(stage, NEAR, IM)
            arrived(stage, BACK, RE)
            take(stage, BACK, RE)

        @pl.when(has_far)
        def _():
            arrived(stage, FAR, IM)
            take_real(stage, FAR, IM)

        after = stage + 1
        more = stage < STAGES - 1

        def piece(half, begin=0):
            part = pl.ds(half * HALF, HALF)
            high, low = split(received(stage, BACK, IM, part))
            columns = [
                left_of[BACK, pl.ds(begin, M), pl.ds(block * M + half * HALF, HALF)]
                for block in range(3)
            ]
            return (
                jnp.concatenate(columns, axis=1),
                jnp.concatenate([high, high, low], axis=0),
                jnp.concatenate([high, high, low], axis=1),
                right_of[BACK, :, pl.ds(begin, M)],
            )

        def sides(half, begin):
            p_part, tall, wide, p_all = piece(half, begin)
            return (
                jnp.dot(p_part, tall, preferred_element_type=F32),
                jnp.dot(wide, p_all, preferred_element_type=F32),
            )

        top, bottom = pl.ds(0, HALF), pl.ds(HALF, HALF)

        def next_real(part, half, slope):
            total[1, part] = slope
            ybuf[after, RE, part] = ybuf[0, RE, part] + ahead * slope
            start(to_back_real(after, ybuf.at[after], half))
            if half == 0:
                far_real(after, ybuf.at[after])

        @pl.when(has_back & more)
        def _():
            arrived(stage, BACK, IM, 0)
            p_part, tall, wide, p_all = piece(0)
            total[1] += jnp.dot(p_part, tall, preferred_element_type=F32)
            total[1, top] -= jnp.dot(wide, p_all, preferred_element_type=F32)
            arrived(stage, BACK, IM, 1)
            p_part, tall, wide, p_all = piece(1)
            left = jnp.dot(p_part[:HALF], tall, preferred_element_type=F32)
            next_real(top, 0, total[1, top] + left)
            left = jnp.dot(p_part[HALF:], tall, preferred_element_type=F32)
            right = jnp.dot(wide, p_all, preferred_element_type=F32)
            next_real(bottom, 1, total[1, bottom] + (left - right))

        @pl.when(has_far & odd_one & jnp.logical_not(more))
        def _():
            take_rest(stage, FAR)

        def finish(half, complex_too):
            part = pl.ds(half * HALF, HALF)
            left, right = sides(half, 0)
            total[1] += left
            total[1, part] -= right
            if complex_too:
                left, right = sides(half, M)
                total[0] -= left
                total[0, part] -= right

        for half in (0, 1):
            @pl.when(has_back & jnp.logical_not(more))
            def _():
                arrived(stage, BACK, IM, half)

            @pl.when(has_back & even & jnp.logical_not(more))
            def _():
                finish(half, True)

            @pl.when(has_back & odd_one & jnp.logical_not(more))
            def _():
                finish(half, False)

        @pl.when(jnp.logical_not(has_back) & more)
        def _():
            ybuf[after, RE] = ybuf[0, RE] + ahead * total[1]
            far_real(after, ybuf.at[after])

        @pl.when(has_back & even & more)
        def _():
            take_rest(stage, BACK)

        @pl.when(has_far & odd_one & more)
        def _():
            take_rest(stage, FAR)

        @pl.when(stage < STAGES - 1)
        def _():
            ybuf[after, IM] = ybuf[0, IM] - ahead * total[0]
            start(to_sibling(after))

    def keep_real(after, ahead):
        zbuf[after, RE] = ybuf[0, RE] + ahead * total[1]

    def keep_imag(after, ahead):
        zbuf[after, IM] = ybuf[0, IM] - ahead * total[0]

    def take_rest(stage, slot):
        left, right = products(slot, received(stage, slot, IM), False, M)
        total[0] -= left + right

    def below_even(stage, ahead):
        after = stage + 1
        arrived(stage, NEAR, IM, 1)
        start(hand_imag(stage, 1))
        arrived(stage, FAR, RE)
        start(hand_real(stage))
        arrived(stage, NEAR, IM, 0)
        start(hand_imag(stage, 0))
        arrived(stage, NEAR, RE)
        take_complex(stage, NEAR, RE)
        take_complex(stage, NEAR, IM)
        arrived(stage, BACK, RE)
        take_complex(stage, BACK, RE)
        arrived(stage, BACK, IM, 0)
        arrived(stage, BACK, IM, 1)
        take_real(stage, BACK, IM)

        @pl.when(stage < STAGES - 1)
        def _():
            keep_real(after, ahead)
            start(to_far_real(after, zbuf.at[after]))

        take_rest(stage, BACK)

        @pl.when(stage < STAGES - 1)
        def _():
            keep_imag(after, ahead)

        take_real(stage, FAR, RE)
        arrived(stage, FAR, IM)
        take_real(stage, FAR, IM)

        @pl.when(stage < STAGES - 1)
        def _():
            ybuf[after, RE] = ybuf[0, RE] + ahead * total[1]
            start(to_back_real(after, ybuf.at[after], 0))
            start(to_back_real(after, ybuf.at[after], 1))
            ybuf[after, IM] = ybuf[0, IM] - ahead * total[0]
            start(to_sibling(after))

    def below_odd(stage, ahead):
        after = stage + 1
        arrived(stage, FAR, RE)
        start(hand_real(stage))
        take_complex(stage, FAR, RE)
        arrived(stage, NEAR, IM, 1)
        start(hand_imag(stage, 1))
        arrived(stage, NEAR, IM, 0)
        start(hand_imag(stage, 0))
        arrived(stage, FAR, IM)
        take_real(stage, FAR, IM)

        @pl.when(stage < STAGES - 1)
        def _():
            keep_real(after, ahead)
            start(to_back_real(after, zbuf.at[after], 0))
            start(to_back_real(after, zbuf.at[after], 1))

        take_rest(stage, FAR)

        @pl.when(stage < STAGES - 1)
        def _():
            keep_imag(after, ahead)
            part_to_sibling(after).start()

        take_real(stage, NEAR, IM)
        arrived(stage, NEAR, RE)
        take_real(stage, NEAR, RE)
        arrived(stage, BACK, RE)
        take_real(stage, BACK, RE)
        arrived(stage, BACK, IM, 0)
        arrived(stage, BACK, IM, 1)
        take_real(stage, BACK, IM)

        @pl.when(stage < STAGES - 1)
        def _():
            ybuf[after, RE] = ybuf[0, RE] + ahead * total[1]
            start(to_far_real(after, ybuf.at[after]))
            ybuf[after, IM] = ybuf[0, IM] - ahead * total[0]
            start(to_sibling(after))

    def late_below(stage):
        @pl.when(even)
        def _():
            part_to_sibling(stage).wait_recv()
            start(to_far_late(stage, zbuf.at[stage], zsib.at[stage]))
            arrived(stage, SIB, IM)

        @pl.when(odd_one)
        def _():
            arrived(stage, SIB, IM)
            start(to_far_late(stage, ybuf.at[stage], win.at[stage, SIB, IM]))

    def stage_body(stage, carry):
        arrived(stage, SIB, RE)
        take(stage, SIB, RE)
        take(stage, SIB, IM)

        @pl.when(above & (stage < STAGES - 1))
        def _():
            contribute(stage)

        ahead = jnp.where(stage == 2, STEP, STEP / 2).astype(F32)

        @pl.when(jnp.logical_not(below))
        def _():
            usual(stage, ahead)

        @pl.when(below & even)
        def _():
            below_even(stage, ahead)

        @pl.when(below & odd_one)
        def _():
            below_odd(stage, ahead)

        @pl.when(stage < STAGES - 1)
        def _():
            weight = jnp.where(stage == 0, 1.0, 2.0).astype(F32)
            acc[RE] += weight * total[1]
            acc[IM] -= weight * total[0]
            own_products(stage + 1, (RE,))

        @pl.when((stage < STAGES - 1) & jnp.logical_not(below))
        def _():
            send_late(stage + 1)

        @pl.when((stage < STAGES - 1) & below)
        def _():
            late_below(stage + 1)

        @pl.when(stage < STAGES - 1)
        def _():
            own_products(stage + 1, (IM,))

        return carry

    lax.fori_loop(0, STAGES, stage_body, 0)

    out[0, RE] = ybuf[0, RE] + (STEP / 6) * (acc[RE] + total[1])
    out[0, IM] = ybuf[0, IM] + (STEP / 6) * (acc[IM] - total[0])

    sent(ybuf, send_sem.at[TO_SIB])

    @pl.when(has_back)
    def _():
        sent(ybuf, send_sem.at[TO_BACK])

    @pl.when(has_far)
    def _():
        sent(win.at[pl.ds(0, 2)], send_sem.at[TO_FAR])

    @pl.when(below & odd_one)
    def _():
        sent(zsib.at[pl.ds(0, STAGES - 1)], z_send)

    @pl.when(below & even)
    def _():
        rim_row(1, FAR).wait_send()

    @pl.when(below & odd_one)
    def _():
        rim_row(0, NEAR).wait_send()
        rim_row(0, BACK).wait_send()


def on_device(
    state, h_static, drive_op, couple, bath_coef, damping, occupation, raise_nbr, lower_nbr
):
    count = lax.axis_size("aux")
    return pl.pallas_call(
        functools.partial(kernel, count),
        out_shape=jax.ShapeDtypeStruct(state.shape, F32),
        in_specs=[pl.BlockSpec(memory_space=pltpu.HBM)] * 9,
        out_specs=pl.BlockSpec(memory_space=pltpu.VMEM),
        scratch_shapes=[
            pltpu.SMEM((2, MODES), F32),
            pltpu.SMEM((MODES,), F32),
            pltpu.SMEM((1, MODES), jnp.int32),
            pltpu.SMEM((1, MODES), jnp.int32),
            pltpu.SMEM((1, MODES), jnp.int32),
            pltpu.VMEM((STAGES, 2, M, M), F32),
            pltpu.VMEM((STAGES, 4, 2, M, M), F32),
            pltpu.VMEM((7, M, M), F32),
            pltpu.VMEM((2, 2, M, M), F32),
            pltpu.VMEM((OWN + 3, 2 * M, 3 * M), BF),
            pltpu.VMEM((OWN + 3, 3 * M, 2 * M), BF),
            pltpu.VMEM((2, M, M), F32),
            pltpu.VMEM((2, M, M), F32),
            pltpu.SMEM((2, 1, MODES), jnp.int32),
            pltpu.VMEM((STAGES, 2, M, M), F32),
            pltpu.VMEM((STAGES, M, M), F32),
            pltpu.VMEM((3, M, 3 * M), BF),
            pltpu.VMEM((3, 3 * M, M), BF),
            pltpu.VMEM((2, 2, 2, M, M), F32),
            pltpu.SemaphoreType.DMA((7,)),
            pltpu.SemaphoreType.DMA((3,)),
            pltpu.SemaphoreType.DMA((STAGES, 10)),
            pltpu.SemaphoreType.DMA((2,)),
            pltpu.SemaphoreType.DMA((2,)),
            pltpu.SemaphoreType.DMA,
            pltpu.SemaphoreType.DMA((STAGES - 1,)),
        ],
        compiler_params=pltpu.CompilerParams(
            collective_id=0, has_side_effects=True, vmem_limit_bytes=48 << 20
        ),
        name="rk_step",
    )(
        *(
            pltpu.with_memory_space_constraint(x, pltpu.HBM)
            for x in (
                bath_coef,
                damping,
                occupation,
                raise_nbr,
                lower_nbr,
                state,
                h_static,
                drive_op,
                couple,
            )
        )
    )


def solution(mesh):
    return jax.shard_map(
        on_device,
        mesh=mesh,
        in_specs=(
            P("aux", None, None, None),
            P(),
            P(),
            P(),
            P(),
            P(),
            P("aux", None),
            P("aux", None),
            P("aux", None),
        ),
        out_specs=P("aux", None, None, None),
        check_vma=False,
    )
```

```python
import functools

import jax
import jax.numpy as jnp
import numpy as np
from jax import lax
from jax.experimental import pallas as pl
from jax.experimental.pallas import tpu as pltpu
from jax.sharding import PartitionSpec as P

MESH = pl.DeviceIdType.MESH
STEP = 0.05
AMP = 2.0
FREQ = 20.0
M = 256
HALF = 128
ROW = 16
MODES = 3
STAGES = 4
SIB, FAR, NEAR, BACK, OWN = range(5)
TO_SIB, TO_BACK, TO_FAR = range(3)
RE, IM = 0, 1
BF = jnp.bfloat16
F32 = jnp.float32


def split(value):
    high = value.astype(BF)
    return high, (value - high.astype(F32)).astype(BF)


def kernel(
    count,
    bath_hbm,
    damp_hbm,
    occ_hbm,
    up_hbm,
    down_hbm,
    state,
    h_static,
    drive_op,
    couple,
    out,
    bath,
    damp,
    occ,
    up,
    down,
    ybuf,
    win,
    raw,
    herm,
    left_of,
    right_of,
    total,
    acc,
    rim,
    zbuf,
    zsib,
    rim_left,
    rim_right,
    extra,
    load_sem,
    send_sem,
    recv_sem,
    sib_recv,
    rim_send,
    rim_recv,
    z_send,
    z_recv,
):
    me = lax.axis_index("aux")
    odd = lax.rem(me, 2)
    even = odd == 0
    d = 1 - 2 * odd

    def at(offset):
        return lax.rem(me + offset + count, count)

    partner = [at(d), at(2 * d), at(-d), at(-2 * d)]
    chip = me // 2
    last = count // 2 - 1
    has_far = (chip + d >= 0) & (chip + d <= last)
    has_back = (chip - d >= 0) & (chip - d <= last)

    below = (lax.rem(chip, ROW) == ROW - 1) & (chip < last)
    above = (lax.rem(chip, ROW) == 0) & (chip > 0)
    odd_one = jnp.logical_not(even)
    across = (below & odd_one) | (above & even)

    moves = [
        (state.at[0], ybuf.at[0]),
        (h_static, raw.at[pl.ds(3, 2)]),
        (drive_op, raw.at[pl.ds(5, 2)]),
        (couple, raw.at[pl.ds(0, 3)]),
        (bath_hbm, bath),
        (damp_hbm, damp),
        (occ_hbm, occ),
        (up_hbm, up),
        (down_hbm, down),
    ]
    barrier = pltpu.get_barrier_semaphore()

    def greet(slot):
        pl.semaphore_signal(
            barrier, inc=1, device_id=(partner[slot],), device_id_type=MESH
        )

    greet(SIB)

    @pl.when(has_far)
    def _():
        greet(FAR)

    @pl.when(has_back)
    def _():
        greet(BACK)

    @pl.when(across)
    def _():
        greet(NEAR)

    loads = [
        pltpu.make_async_copy(src, dst, load_sem.at[max(i, 3) - 3 if i else 6])
        for i, (src, dst) in enumerate(moves)
    ]
    for load in loads:
        load.start()

    pl.semaphore_wait(
        barrier,
        1
        + jnp.where(has_far, 1, 0)
        + jnp.where(has_back, 1, 0)
        + jnp.where(across, 1, 0),
    )

    def rows(ref, half):
        return ref if half is None else ref.at[pl.ds(half * HALF, HALF)]

    def flag(stage, slot, plane, half):
        number = {
            (SIB, RE): 0,
            (SIB, IM): 1,
            (FAR, RE): 2,
            (FAR, IM): 3,
            (NEAR, RE): 4,
            (NEAR, IM): 5 + (half or 0),
            (BACK, RE): 7,
            (BACK, IM): 8 + (half or 0),
        }[slot, plane]
        if slot == SIB:
            return sib_recv.at[lax.rem(stage, 2), number]
        return recv_sem.at[lax.rem(stage, 3), number - 2]

    def remote(src, stage, slot, plane, half, group, device):
        return pltpu.make_async_remote_copy(
            src_ref=rows(src, half),
            dst_ref=rows(win.at[stage, slot, plane], half),
            send_sem=send_sem.at[group],
            recv_sem=flag(stage, slot, plane, half),
            device_id=(device,),
            device_id_type=MESH,
        )

    def to_back_real(stage, own, half):
        return [remote(own.at[RE], stage, FAR, RE, half, TO_BACK, partner[BACK])]

    def to_far_real(stage, own):
        return [remote(own.at[RE], stage, BACK, RE, 0, TO_FAR, partner[FAR])]

    def to_far_late(stage, own, other):
        return [
            remote(other, stage, NEAR, IM, 1, TO_FAR, partner[FAR]),
            remote(other, stage, NEAR, IM, 0, TO_FAR, partner[FAR]),
            remote(own.at[RE], stage, BACK, RE, 1, TO_FAR, partner[FAR]),
            remote(own.at[IM], stage, BACK, IM, 0, TO_FAR, partner[FAR]),
            remote(own.at[IM], stage, BACK, IM, 1, TO_FAR, partner[FAR]),
        ]

    def to_sibling(stage):
        return [
            remote(ybuf.at[stage, IM], stage, SIB, IM, None, TO_SIB, partner[SIB]),
            remote(ybuf.at[stage, RE], stage, SIB, RE, None, TO_SIB, partner[SIB]),
        ]

    def part_to_sibling(stage):
        return pltpu.make_async_remote_copy(
            src_ref=zbuf.at[stage, IM],
            dst_ref=zsib.at[stage],
            send_sem=z_send,
            recv_sem=z_recv.at[stage - 1],
            device_id=(partner[SIB],),
            device_id_type=MESH,
        )

    def rim_row(i, slot):
        return pltpu.make_async_remote_copy(
            src_ref=up_hbm,
            dst_ref=rim.at[i],
            send_sem=rim_send.at[0 if slot != BACK else 1],
            recv_sem=rim_recv.at[i],
            device_id=(partner[slot],),
            device_id_type=MESH,
        )

    def hand_real(stage):
        return [remote(win.at[stage, FAR, RE], stage, NEAR, RE, None, TO_FAR, partner[SIB])]

    def hand_imag(stage, half):
        return [remote(win.at[stage, NEAR, IM], stage, FAR, IM, half, TO_BACK, partner[SIB])]

    def start(copies):
        for copy in copies:
            copy.start()

    def back_real(stage, own):
        @pl.when(has_back)
        def _():
            start(to_back_real(stage, own, 0))
            start(to_back_real(stage, own, 1))

    def far_real(stage, own):
        @pl.when(has_far)
        def _():
            start(to_far_real(stage, own))

    def arrived(stage, slot, plane, half=None):
        remote(
            win.at[stage, slot, plane], stage, slot, plane, half, TO_SIB, partner[SIB]
        ).wait_recv()

    def sent(ref, sem):
        pltpu.make_async_remote_copy(
            src_ref=ref,
            dst_ref=ref,
            send_sem=sem,
            recv_sem=z_recv.at[0],
            device_id=(partner[SIB],),
            device_id_type=MESH,
        ).wait_send()

    def late_far(stage, own, other):
        @pl.when(has_far)
        def _():
            start(to_far_late(stage, own, other))

    def send_late(stage):
        arrived(stage, SIB, IM)
        late_far(stage, ybuf.at[stage], win.at[stage, SIB, IM])

    loads[0].wait()
    back_real(0, ybuf.at[0])
    far_real(0, ybuf.at[0])
    start(to_sibling(0))

    @pl.when(below & even)
    def _():
        rim_row(1, FAR).start()

    @pl.when(below & odd_one)
    def _():
        rim_row(0, NEAR).start()
        rim_row(0, BACK).start()

    def put(slot, real, imag, imag_right):
        for row, value in ((0, real), (M, imag)):
            high, low = split(value)
            left_of[slot, pl.ds(row, M), pl.ds(0, M)] = high
            left_of[slot, pl.ds(row, M), pl.ds(M, M)] = low
            left_of[slot, pl.ds(row, M), pl.ds(2 * M, M)] = high
        for column, value in ((0, real), (M, imag_right)):
            high, low = split(value)
            right_of[slot, pl.ds(0, M), pl.ds(column, M)] = high
            right_of[slot, pl.ds(M, M), pl.ds(column, M)] = low
            right_of[slot, pl.ds(2 * M, M), pl.ds(column, M)] = high

    def products(slot, value, wide, begin=0):
        high, low = split(value)
        size = 2 * M if wide else M
        left = jnp.dot(
            left_of[slot, pl.ds(begin, size)],
            jnp.concatenate([high, high, low], axis=0),
            preferred_element_type=F32,
        )
        right = jnp.dot(
            jnp.concatenate([high, high, low], axis=1),
            right_of[slot, :, pl.ds(begin, size)],
            preferred_element_type=F32,
        )
        return left, right

    def own_products(stage, planes):
        slot = OWN + (stage + 1) // 2
        real, imag = ybuf[stage, RE], ybuf[stage, IM]
        if RE in planes:
            left, right = products(slot, real, True)
            total[0] = rate * imag + (left[:M] - right[:, :M])
            total[1] = (left[M:] + right[:, M:]) - rate * real
        if IM in planes:
            left, right = products(slot, imag, True)
            total[0] -= left[M:] + right[:, M:]
            total[1] += left[:M] - right[:, :M]

    def received(stage, slot, plane, part=pl.ds(0, M)):
        value = win[stage, slot, plane, part]
        if slot == SIB:
            return value
        who = odd_one if slot == FAR else even
        before = jnp.where(stage == STAGES - 1, STEP, STEP / 2).astype(F32)
        scale = jnp.where(above & who & (stage > 0), before, 0.0).astype(F32)
        which = 1 if slot == BACK else 0
        other = extra[lax.rem(stage, 2), which, 1 - plane, part]
        return value + (scale if plane == RE else -scale) * other

    def take_complex(stage, slot, plane):
        left, right = products(slot, received(stage, slot, plane), True)
        minus = left[:M] - right[:, :M]
        plus = left[M:] + right[:, M:]
        if plane == RE:
            total[0] += minus
            total[1] += plus
        else:
            total[0] -= plus
            total[1] += minus

    def take_real(stage, slot, plane):
        left, right = products(slot, received(stage, slot, plane), False)
        total[plane] += left - right

    def contribution(i, value):
        high, low = split(value)
        left = jnp.dot(
            rim_left[i],
            jnp.concatenate([high, high, low], axis=0),
            preferred_element_type=F32,
        )
        right = jnp.dot(
            jnp.concatenate([high, high, low], axis=1),
            rim_right[i],
            preferred_element_type=F32,
        )
        return left - right

    def contribute(stage):
        later = lax.rem(stage + 1, 2)
        for plane in (RE, IM):
            own = ybuf[stage, plane]
            extra[later, 0, plane] = contribution(0, own) + contribution(
                1, win[stage, SIB, plane]
            )

        @pl.when(even)
        def _():
            for plane in (RE, IM):
                extra[later, 1, plane] = contribution(2, ybuf[stage, plane])

    def take(stage, slot, plane):
        real = even if slot in (SIB, FAR) else jnp.logical_not(even)

        @pl.when(real)
        def _():
            take_real(stage, slot, plane)

        @pl.when(jnp.logical_not(real))
        def _():
            take_complex(stage, slot, plane)

    drive = [
        np.float32(AMP) * np.cos(np.float32(FREQ * t)) for t in (0.0, STEP / 2, STEP)
    ]

    def put_own(i):
        real = herm[0, 0] + drive[i] * herm[1, 0]
        imag = herm[0, 1] + drive[i] * herm[1, 1]
        put(OWN + i, real, imag, -imag)

    for load in loads[4:]:
        load.wait()
    rate = jnp.float32(0.0)
    for k in range(MODES):
        rate = rate + occ[0, k].astype(F32) * damp[k]

    pltpu.make_async_copy(raw, raw, load_sem.at[0]).wait()
    for k in range(2):
        value = raw[3 + 2 * k]
        herm[k, 0] = (value + value.T) * 0.5
        value = raw[4 + 2 * k]
        herm[k, 1] = (value - value.T) * 0.5
    put_own(0)
    own_products(0, (RE, IM))
    send_late(0)

    for k in range(MODES):
        value = raw[k]
        raw[k] = (value + value.T) * 0.5

    for slot in range(4):
        real = jnp.zeros((M, M), F32)
        imag = jnp.zeros((M, M), F32)
        for k in range(MODES):
            raises = jnp.where(up[0, k] == partner[slot], 1.0, 0.0).astype(F32)
            lowers = jnp.where(
                down[0, k] == partner[slot], occ[0, k].astype(F32), 0.0
            ).astype(F32)
            real = real + (raises + lowers * bath[0, k]) * raw[k]
            imag = imag + (lowers * bath[1, k]) * raw[k]
        put(slot, real, imag, imag)

    put_own(1)
    put_own(2)
    acc[...] = jnp.zeros_like(acc)
    extra[...] = jnp.zeros_like(extra)

    def put_rim(i, row, source):
        real = jnp.zeros((M, M), F32)
        for k in range(MODES):
            real = real + jnp.where(rim[row, 0, k] == source, 1.0, 0.0).astype(F32) * raw[k]
        high, low = split(real)
        for j, part in enumerate((high, low, high)):
            rim_left[i, :, pl.ds(j * M, M)] = part
            rim_right[i, pl.ds(j * M, M), :] = part

    @pl.when(above)
    def _():
        rim_row(0, NEAR).wait_recv()
        put_rim(0, 0, me)
        put_rim(1, 0, partner[SIB])

    @pl.when(above & even)
    def _():
        rim_row(1, NEAR).wait_recv()
        put_rim(2, 1, me)

    def usual(stage, ahead):
        @pl.when(has_far)
        def _():
            arrived(stage, FAR, RE)
            start(hand_real(stage))

        @pl.when(has_back)
        def _():
            arrived(stage, NEAR, IM, 1)
            start(hand_imag(stage, 1))

        @pl.when(has_far)
        def _():
            take(stage, FAR, RE)

        @pl.when(has_back)
        def _():
            arrived(stage, NEAR, IM, 0)
            start(hand_imag(stage, 0))
            arrived(stage, NEAR, RE)
            take(stage, NEAR, RE)
            take(stage, NEAR, IM)
            arrived(stage, BACK, RE)
            take(stage, BACK, RE)

        @pl.when(has_far)
        def _():
            arrived(stage, FAR, IM)
            take_real(stage, FAR, IM)

        after = stage + 1
        more = stage < STAGES - 1

        def piece(half, begin=0):
            part = pl.ds(half * HALF, HALF)
            high, low = split(received(stage, BACK, IM, part))
            columns = [
                left_of[BACK, pl.ds(begin, M), pl.ds(block * M + half * HALF, HALF)]
                for block in range(3)
            ]
            return (
                jnp.concatenate(columns, axis=1),
                jnp.concatenate([high, high, low], axis=0),
                jnp.concatenate([high, high, low], axis=1),
                right_of[BACK, :, pl.ds(begin, M)],
            )

        def sides(half, begin):
            p_part, tall, wide, p_all = piece(half, begin)
            return (
                jnp.dot(p_part, tall, preferred_element_type=F32),
                jnp.dot(wide, p_all, preferred_element_type=F32),
            )

        top, bottom = pl.ds(0, HALF), pl.ds(HALF, HALF)

        def next_real(part, half, slope):
            total[1, part] = slope
            ybuf[after, RE, part] = ybuf[0, RE, part] + ahead * slope
            start(to_back_real(after, ybuf.at[after], half))
            if half == 0:
                far_real(after, ybuf.at[after])

        @pl.when(has_back & more)
        def _():
            arrived(stage, BACK, IM, 0)
            p_part, tall, wide, p_all = piece(0)
            total[1] += jnp.dot(p_part, tall, preferred_element_type=F32)
            total[1, top] -= jnp.dot(wide, p_all, preferred_element_type=F32)
            arrived(stage, BACK, IM, 1)
            p_part, tall, wide, p_all = piece(1)
            left = jnp.dot(p_part[:HALF], tall, preferred_element_type=F32)
            next_real(top, 0, total[1, top] + left)
            left = jnp.dot(p_part[HALF:], tall, preferred_element_type=F32)
            right = jnp.dot(wide, p_all, preferred_element_type=F32)
            next_real(bottom, 1, total[1, bottom] + (left - right))

        @pl.when(has_far & odd_one & jnp.logical_not(more))
        def _():
            take_rest(stage, FAR)

        def finish(half, complex_too):
            part = pl.ds(half * HALF, HALF)
            left, right = sides(half, 0)
            total[1] += left
            total[1, part] -= right
            if complex_too:
                left, right = sides(half, M)
                total[0] -= left
                total[0, part] -= right

        for half in (0, 1):
            @pl.when(has_back & jnp.logical_not(more))
            def _():
                arrived(stage, BACK, IM, half)

            @pl.when(has_back & even & jnp.logical_not(more))
            def _():
                finish(half, True)

            @pl.when(has_back & odd_one & jnp.logical_not(more))
            def _():
                finish(half, False)

        @pl.when(jnp.logical_not(has_back) & more)
        def _():
            ybuf[after, RE] = ybuf[0, RE] + ahead * total[1]
            far_real(after, ybuf.at[after])

        @pl.when(has_back & even & more)
        def _():
            take_rest(stage, BACK)

        @pl.when(has_far & odd_one & more)
        def _():
            take_rest(stage, FAR)

        @pl.when(stage < STAGES - 1)
        def _():
            ybuf[after, IM] = ybuf[0, IM] - ahead * total[0]
            start(to_sibling(after))

    def keep_real(after, ahead):
        zbuf[after, RE] = ybuf[0, RE] + ahead * total[1]

    def keep_imag(after, ahead):
        zbuf[after, IM] = ybuf[0, IM] - ahead * total[0]

    def take_rest(stage, slot):
        left, right = products(slot, received(stage, slot, IM), False, M)
        total[0] -= left + right

    def below_even(stage, ahead):
        after = stage + 1
        arrived(stage, NEAR, IM, 1)
        start(hand_imag(stage, 1))
        arrived(stage, FAR, RE)
        start(hand_real(stage))
        arrived(stage, NEAR, IM, 0)
        start(hand_imag(stage, 0))
        arrived(stage, NEAR, RE)
        take_complex(stage, NEAR, RE)
        take_complex(stage, NEAR, IM)
        arrived(stage, BACK, RE)
        take_complex(stage, BACK, RE)
        arrived(stage, BACK, IM, 0)
        arrived(stage, BACK, IM, 1)
        take_real(stage, BACK, IM)

        @pl.when(stage < STAGES - 1)
        def _():
            keep_real(after, ahead)
            start(to_far_real(after, zbuf.at[after]))

        take_rest(stage, BACK)

        @pl.when(stage < STAGES - 1)
        def _():
            keep_imag(after, ahead)

        take_real(stage, FAR, RE)
        arrived(stage, FAR, IM)
        take_real(stage, FAR, IM)

        @pl.when(stage < STAGES - 1)
        def _():
            ybuf[after, RE] = ybuf[0, RE] + ahead * total[1]
            start(to_back_real(after, ybuf.at[after], 0))
            start(to_back_real(after, ybuf.at[after], 1))
            ybuf[after, IM] = ybuf[0, IM] - ahead * total[0]
            start(to_sibling(after))

    def below_odd(stage, ahead):
        after = stage + 1
        arrived(stage, FAR, RE)
        start(hand_real(stage))
        take_complex(stage, FAR, RE)
        arrived(stage, NEAR, IM, 1)
        start(hand_imag(stage, 1))
        arrived(stage, NEAR, IM, 0)
        start(hand_imag(stage, 0))
        arrived(stage, FAR, IM)
        take_real(stage, FAR, IM)

        @pl.when(stage < STAGES - 1)
        def _():
            keep_real(after, ahead)
            start(to_back_real(after, zbuf.at[after], 0))
            start(to_back_real(after, zbuf.at[after], 1))

        take_rest(stage, FAR)

        @pl.when(stage < STAGES - 1)
        def _():
            keep_imag(after, ahead)
            part_to_sibling(after).start()

        take_real(stage, NEAR, IM)
        arrived(stage, NEAR, RE)
        take_real(stage, NEAR, RE)
        arrived(stage, BACK, RE)
        take_real(stage, BACK, RE)
        arrived(stage, BACK, IM, 0)
        arrived(stage, BACK, IM, 1)
        take_real(stage, BACK, IM)

        @pl.when(stage < STAGES - 1)
        def _():
            ybuf[after, RE] = ybuf[0, RE] + ahead * total[1]
            start(to_far_real(after, ybuf.at[after]))
            ybuf[after, IM] = ybuf[0, IM] - ahead * total[0]
            start(to_sibling(after))

    def late_below(stage):
        @pl.when(even)
        def _():
            part_to_sibling(stage).wait_recv()
            start(to_far_late(stage, zbuf.at[stage], zsib.at[stage]))
            arrived(stage, SIB, IM)

        @pl.when(odd_one)
        def _():
            arrived(stage, SIB, IM)
            start(to_far_late(stage, ybuf.at[stage], win.at[stage, SIB, IM]))

    def stage_body(stage, carry):
        arrived(stage, SIB, RE)
        take(stage, SIB, RE)
        take(stage, SIB, IM)

        @pl.when(above & (stage < STAGES - 1))
        def _():
            contribute(stage)

        ahead = jnp.where(stage == 2, STEP, STEP / 2).astype(F32)

        @pl.when(jnp.logical_not(below))
        def _():
            usual(stage, ahead)

        @pl.when(below & even)
        def _():
            below_even(stage, ahead)

        @pl.when(below & odd_one)
        def _():
            below_odd(stage, ahead)

        @pl.when(stage < STAGES - 1)
        def _():
            weight = jnp.where(stage == 0, 1.0, 2.0).astype(F32)
            acc[RE] += weight * total[1]
            acc[IM] -= weight * total[0]
            own_products(stage + 1, (RE,))

        @pl.when((stage < STAGES - 1) & jnp.logical_not(below))
        def _():
            send_late(stage + 1)

        @pl.when((stage < STAGES - 1) & below)
        def _():
            late_below(stage + 1)

        @pl.when(stage < STAGES - 1)
        def _():
            own_products(stage + 1, (IM,))

        return carry

    lax.fori_loop(0, STAGES, stage_body, 0)

    out[0, RE] = ybuf[0, RE] + (STEP / 6) * (acc[RE] + total[1])
    out[0, IM] = ybuf[0, IM] + (STEP / 6) * (acc[IM] - total[0])

    sent(ybuf, send_sem.at[TO_SIB])

    @pl.when(has_back)
    def _():
        sent(ybuf, send_sem.at[TO_BACK])

    @pl.when(has_far)
    def _():
        sent(win.at[pl.ds(0, 2)], send_sem.at[TO_FAR])

    @pl.when(below & odd_one)
    def _():
        sent(zsib.at[pl.ds(0, STAGES - 1)], z_send)

    @pl.when(below & even)
    def _():
        rim_row(1, FAR).wait_send()

    @pl.when(below & odd_one)
    def _():
        rim_row(0, NEAR).wait_send()
        rim_row(0, BACK).wait_send()


def on_device(
    state, h_static, drive_op, couple, bath_coef, damping, occupation, raise_nbr, lower_nbr
):
    count = lax.axis_size("aux")
    return pl.pallas_call(
        functools.partial(kernel, count),
        out_shape=jax.ShapeDtypeStruct(state.shape, F32),
        in_specs=[pl.BlockSpec(memory_space=pltpu.HBM)] * 9,
        out_specs=pl.BlockSpec(memory_space=pltpu.VMEM),
        scratch_shapes=[
            pltpu.SMEM((2, MODES), F32),
            pltpu.SMEM((MODES,), F32),
            pltpu.SMEM((1, MODES), jnp.int32),
            pltpu.SMEM((1, MODES), jnp.int32),
            pltpu.SMEM((1, MODES), jnp.int32),
            pltpu.VMEM((STAGES, 2, M, M), F32),
            pltpu.VMEM((STAGES, 4, 2, M, M), F32),
            pltpu.VMEM((7, M, M), F32),
            pltpu.VMEM((2, 2, M, M), F32),
            pltpu.VMEM((OWN + 3, 2 * M, 3 * M), BF),
            pltpu.VMEM((OWN + 3, 3 * M, 2 * M), BF),
            pltpu.VMEM((2, M, M), F32),
            pltpu.VMEM((2, M, M), F32),
            pltpu.SMEM((2, 1, MODES), jnp.int32),
            pltpu.VMEM((STAGES, 2, M, M), F32),
            pltpu.VMEM((STAGES, M, M), F32),
            pltpu.VMEM((3, M, 3 * M), BF),
            pltpu.VMEM((3, 3 * M, M), BF),
            pltpu.VMEM((2, 2, 2, M, M), F32),
            pltpu.SemaphoreType.DMA((7,)),
            pltpu.SemaphoreType.DMA((3,)),
            pltpu.SemaphoreType.DMA((3, 8)),
            pltpu.SemaphoreType.DMA((2, 2)),
            pltpu.SemaphoreType.DMA((2,)),
            pltpu.SemaphoreType.DMA((2,)),
            pltpu.SemaphoreType.DMA,
            pltpu.SemaphoreType.DMA((STAGES - 1,)),
        ],
        compiler_params=pltpu.CompilerParams(
            collective_id=0, has_side_effects=True, vmem_limit_bytes=48 << 20
        ),
        name="rk_step",
    )(
        *(
            pltpu.with_memory_space_constraint(x, pltpu.HBM)
            for x in (
                bath_coef,
                damping,
                occupation,
                raise_nbr,
                lower_nbr,
                state,
                h_static,
                drive_op,
                couple,
            )
        )
    )


def solution(mesh):
    return jax.shard_map(
        on_device,
        mesh=mesh,
        in_specs=(
            P("aux", None, None, None),
            P(),
            P(),
            P(),
            P(),
            P(),
            P("aux", None),
            P("aux", None),
            P("aux", None),
        ),
        out_specs=P("aux", None, None, None),
        check_vma=False,
    )
```

```python
import functools

import jax
import jax.numpy as jnp
import numpy as np
from jax import lax
from jax.experimental import pallas as pl
from jax.experimental.pallas import tpu as pltpu
from jax.sharding import PartitionSpec as P

MESH = pl.DeviceIdType.MESH
STEP = 0.05
AMP = 2.0
FREQ = 20.0
M = 256
HALF = 128
ROW = 16
MODES = 3
STAGES = 4
SIB, FAR, NEAR, BACK, OWN = range(5)
TO_SIB, TO_BACK, TO_FAR = range(3)
RE, IM = 0, 1
BF = jnp.bfloat16
F32 = jnp.float32


def split(value):
    high = value.astype(BF)
    return high, (value - high.astype(F32)).astype(BF)


def kernel(
    count,
    bath_hbm,
    damp_hbm,
    occ_hbm,
    up_hbm,
    down_hbm,
    state,
    h_static,
    drive_op,
    couple,
    out,
    bath,
    damp,
    occ,
    up,
    down,
    ybuf,
    win,
    raw,
    herm,
    left_of,
    right_of,
    total,
    acc,
    rim,
    zbuf,
    zsib,
    rim_left,
    rim_right,
    extra,
    load_sem,
    send_sem,
    recv_sem,
    sib_recv,
    rim_send,
    rim_recv,
    z_send,
    z_recv,
):
    me = lax.axis_index("aux")
    odd = lax.rem(me, 2)
    even = odd == 0
    d = 1 - 2 * odd

    def at(offset):
        return lax.rem(me + offset + count, count)

    partner = [at(d), at(2 * d), at(-d), at(-2 * d)]
    chip = me // 2
    last = count // 2 - 1
    has_far = (chip + d >= 0) & (chip + d <= last)
    has_back = (chip - d >= 0) & (chip - d <= last)

    below = (lax.rem(chip, ROW) == ROW - 1) & (chip < last)
    above = (lax.rem(chip, ROW) == 0) & (chip > 0)
    odd_one = jnp.logical_not(even)
    across = (below & odd_one) | (above & even)

    moves = [
        (state.at[0], ybuf.at[0]),
        (h_static, raw.at[pl.ds(3, 2)]),
        (drive_op, raw.at[pl.ds(5, 2)]),
        (couple, raw.at[pl.ds(0, 3)]),
        (bath_hbm, bath),
        (damp_hbm, damp),
        (occ_hbm, occ),
        (up_hbm, up),
        (down_hbm, down),
    ]
    barrier = pltpu.get_barrier_semaphore()

    def greet(slot):
        pl.semaphore_signal(
            barrier, inc=1, device_id=(partner[slot],), device_id_type=MESH
        )

    greet(SIB)

    @pl.when(has_far)
    def _():
        greet(FAR)

    @pl.when(has_back)
    def _():
        greet(BACK)

    @pl.when(across)
    def _():
        greet(NEAR)

    loads = [
        pltpu.make_async_copy(src, dst, load_sem.at[max(i, 3) - 3 if i else 6])
        for i, (src, dst) in enumerate(moves)
    ]
    for load in loads:
        load.start()

    pl.semaphore_wait(
        barrier,
        1
        + jnp.where(has_far, 1, 0)
        + jnp.where(has_back, 1, 0)
        + jnp.where(across, 1, 0),
    )

    def rows(ref, half):
        return ref if half is None else ref.at[pl.ds(half * HALF, HALF)]

    def flag(stage, slot, plane, half):
        number = {
            (SIB, RE): 0,
            (SIB, IM): 1,
            (FAR, RE): 2 if half == 1 else 10,
            (FAR, IM): 3,
            (NEAR, RE): 4,
            (NEAR, IM): 5 + (half or 0),
            (BACK, RE): 7,
            (BACK, IM): 8 + (half or 0),
        }[slot, plane]
        if slot == SIB:
            return sib_recv.at[lax.rem(stage, 2), number]
        return recv_sem.at[lax.rem(stage, 3), number - 2]

    def remote(src, stage, slot, plane, half, group, device):
        return pltpu.make_async_remote_copy(
            src_ref=rows(src, half),
            dst_ref=rows(win.at[stage, slot, plane], half),
            send_sem=send_sem.at[group],
            recv_sem=flag(stage, slot, plane, half),
            device_id=(device,),
            device_id_type=MESH,
        )

    def to_back_real(stage, own, half):
        return [remote(own.at[RE], stage, FAR, RE, half, TO_BACK, partner[BACK])]

    def to_far_real(stage, own):
        return [remote(own.at[RE], stage, BACK, RE, 0, TO_FAR, partner[FAR])]

    def to_far_late(stage, own, other):
        return [
            remote(other, stage, NEAR, IM, 1, TO_FAR, partner[FAR]),
            remote(other, stage, NEAR, IM, 0, TO_FAR, partner[FAR]),
            remote(own.at[RE], stage, BACK, RE, 1, TO_FAR, partner[FAR]),
            remote(own.at[IM], stage, BACK, IM, 0, TO_FAR, partner[FAR]),
            remote(own.at[IM], stage, BACK, IM, 1, TO_FAR, partner[FAR]),
        ]

    def to_sibling(stage):
        return [
            remote(ybuf.at[stage, IM], stage, SIB, IM, None, TO_SIB, partner[SIB]),
            remote(ybuf.at[stage, RE], stage, SIB, RE, None, TO_SIB, partner[SIB]),
        ]

    def part_to_sibling(stage):
        return pltpu.make_async_remote_copy(
            src_ref=zbuf.at[stage, IM],
            dst_ref=zsib.at[stage],
            send_sem=z_send,
            recv_sem=z_recv.at[stage - 1],
            device_id=(partner[SIB],),
            device_id_type=MESH,
        )

    def rim_row(i, slot):
        return pltpu.make_async_remote_copy(
            src_ref=up_hbm,
            dst_ref=rim.at[i],
            send_sem=rim_send.at[0 if slot != BACK else 1],
            recv_sem=rim_recv.at[i],
            device_id=(partner[slot],),
            device_id_type=MESH,
        )

    def hand_real(stage, half):
        return [remote(win.at[stage, FAR, RE], stage, NEAR, RE, half, TO_FAR, partner[SIB])]

    def hand_imag(stage, half):
        return [remote(win.at[stage, NEAR, IM], stage, FAR, IM, half, TO_BACK, partner[SIB])]

    def start(copies):
        for copy in copies:
            copy.start()

    def back_real(stage, own):
        @pl.when(has_back)
        def _():
            start(to_back_real(stage, own, 0))
            start(to_back_real(stage, own, 1))

    def far_real(stage, own):
        @pl.when(has_far)
        def _():
            start(to_far_real(stage, own))

    def arrived(stage, slot, plane, half=None):
        remote(
            win.at[stage, slot, plane], stage, slot, plane, half, TO_SIB, partner[SIB]
        ).wait_recv()

    def sent(ref, sem):
        pltpu.make_async_remote_copy(
            src_ref=ref,
            dst_ref=ref,
            send_sem=sem,
            recv_sem=z_recv.at[0],
            device_id=(partner[SIB],),
            device_id_type=MESH,
        ).wait_send()

    def late_far(stage, own, other):
        @pl.when(has_far)
        def _():
            start(to_far_late(stage, own, other))

    def send_late(stage):
        arrived(stage, SIB, IM)
        late_far(stage, ybuf.at[stage], win.at[stage, SIB, IM])

    loads[0].wait()
    back_real(0, ybuf.at[0])
    far_real(0, ybuf.at[0])
    start(to_sibling(0))

    @pl.when(below & even)
    def _():
        rim_row(1, FAR).start()

    @pl.when(below & odd_one)
    def _():
        rim_row(0, NEAR).start()
        rim_row(0, BACK).start()

    def put(slot, real, imag, imag_right):
        for row, value in ((0, real), (M, imag)):
            high, low = split(value)
            left_of[slot, pl.ds(row, M), pl.ds(0, M)] = high
            left_of[slot, pl.ds(row, M), pl.ds(M, M)] = low
            left_of[slot, pl.ds(row, M), pl.ds(2 * M, M)] = high
        for column, value in ((0, real), (M, imag_right)):
            high, low = split(value)
            right_of[slot, pl.ds(0, M), pl.ds(column, M)] = high
            right_of[slot, pl.ds(M, M), pl.ds(column, M)] = low
            right_of[slot, pl.ds(2 * M, M), pl.ds(column, M)] = high

    def products(slot, value, wide, begin=0):
        high, low = split(value)
        size = 2 * M if wide else M
        left = jnp.dot(
            left_of[slot, pl.ds(begin, size)],
            jnp.concatenate([high, high, low], axis=0),
            preferred_element_type=F32,
        )
        right = jnp.dot(
            jnp.concatenate([high, high, low], axis=1),
            right_of[slot, :, pl.ds(begin, size)],
            preferred_element_type=F32,
        )
        return left, right

    def own_products(stage, planes):
        slot = OWN + (stage + 1) // 2
        real, imag = ybuf[stage, RE], ybuf[stage, IM]
        if RE in planes:
            left, right = products(slot, real, True)
            total[0] = rate * imag + (left[:M] - right[:, :M])
            total[1] = (left[M:] + right[:, M:]) - rate * real
        if IM in planes:
            left, right = products(slot, imag, True)
            total[0] -= left[M:] + right[:, M:]
            total[1] += left[:M] - right[:, :M]

    def received(stage, slot, plane, part=pl.ds(0, M)):
        value = win[stage, slot, plane, part]
        if slot == SIB:
            return value
        who = odd_one if slot == FAR else even
        before = jnp.where(stage == STAGES - 1, STEP, STEP / 2).astype(F32)
        scale = jnp.where(above & who & (stage > 0), before, 0.0).astype(F32)
        which = 1 if slot == BACK else 0
        other = extra[lax.rem(stage, 2), which, 1 - plane, part]
        return value + (scale if plane == RE else -scale) * other

    def take_complex(stage, slot, plane):
        left, right = products(slot, received(stage, slot, plane), True)
        minus = left[:M] - right[:, :M]
        plus = left[M:] + right[:, M:]
        if plane == RE:
            total[0] += minus
            total[1] += plus
        else:
            total[0] -= plus
            total[1] += minus

    def take_real(stage, slot, plane):
        left, right = products(slot, received(stage, slot, plane), False)
        total[plane] += left - right

    def contribution(i, value):
        high, low = split(value)
        left = jnp.dot(
            rim_left[i],
            jnp.concatenate([high, high, low], axis=0),
            preferred_element_type=F32,
        )
        right = jnp.dot(
            jnp.concatenate([high, high, low], axis=1),
            rim_right[i],
            preferred_element_type=F32,
        )
        return left - right

    def contribute(stage):
        later = lax.rem(stage + 1, 2)
        for plane in (RE, IM):
            own = ybuf[stage, plane]
            extra[later, 0, plane] = contribution(0, own) + contribution(
                1, win[stage, SIB, plane]
            )

        @pl.when(even)
        def _():
            for plane in (RE, IM):
                extra[later, 1, plane] = contribution(2, ybuf[stage, plane])

    def take(stage, slot, plane):
        real = even if slot in (SIB, FAR) else jnp.logical_not(even)

        @pl.when(real)
        def _():
            take_real(stage, slot, plane)

        @pl.when(jnp.logical_not(real))
        def _():
            take_complex(stage, slot, plane)

    drive = [
        np.float32(AMP) * np.cos(np.float32(FREQ * t)) for t in (0.0, STEP / 2, STEP)
    ]

    def put_own(i):
        real = herm[0, 0] + drive[i] * herm[1, 0]
        imag = herm[0, 1] + drive[i] * herm[1, 1]
        put(OWN + i, real, imag, -imag)

    for load in loads[4:]:
        load.wait()
    rate = jnp.float32(0.0)
    for k in range(MODES):
        rate = rate + occ[0, k].astype(F32) * damp[k]

    pltpu.make_async_copy(raw, raw, load_sem.at[0]).wait()
    for k in range(2):
        value = raw[3 + 2 * k]
        herm[k, 0] = (value + value.T) * 0.5
        value = raw[4 + 2 * k]
        herm[k, 1] = (value - value.T) * 0.5
    put_own(0)
    own_products(0, (RE, IM))
    send_late(0)

    for k in range(MODES):
        value = raw[k]
        raw[k] = (value + value.T) * 0.5

    for slot in range(4):
        real = jnp.zeros((M, M), F32)
        imag = jnp.zeros((M, M), F32)
        for k in range(MODES):
            raises = jnp.where(up[0, k] == partner[slot], 1.0, 0.0).astype(F32)
            lowers = jnp.where(
                down[0, k] == partner[slot], occ[0, k].astype(F32), 0.0
            ).astype(F32)
            real = real + (raises + lowers * bath[0, k]) * raw[k]
            imag = imag + (lowers * bath[1, k]) * raw[k]
        put(slot, real, imag, imag)

    put_own(1)
    put_own(2)
    acc[...] = jnp.zeros_like(acc)
    extra[...] = jnp.zeros_like(extra)

    def put_rim(i, row, source):
        real = jnp.zeros((M, M), F32)
        for k in range(MODES):
            real = real + jnp.where(rim[row, 0, k] == source, 1.0, 0.0).astype(F32) * raw[k]
        high, low = split(real)
        for j, part in enumerate((high, low, high)):
            rim_left[i, :, pl.ds(j * M, M)] = part
            rim_right[i, pl.ds(j * M, M), :] = part

    @pl.when(above)
    def _():
        rim_row(0, NEAR).wait_recv()
        put_rim(0, 0, me)
        put_rim(1, 0, partner[SIB])

    @pl.when(above & even)
    def _():
        rim_row(1, NEAR).wait_recv()
        put_rim(2, 1, me)

    def usual(stage, ahead):
        @pl.when(has_far)
        def _():
            arrived(stage, FAR, RE, 0)
            start(hand_real(stage, 0))
            arrived(stage, FAR, RE, 1)
            start(hand_real(stage, 1))

        @pl.when(has_back)
        def _():
            arrived(stage, NEAR, IM, 1)
            start(hand_imag(stage, 1))

        @pl.when(has_far)
        def _():
            take(stage, FAR, RE)

        @pl.when(has_back)
        def _():
            arrived(stage, NEAR, IM, 0)
            start(hand_imag(stage, 0))
            arrived(stage, NEAR, RE)
            take(stage, NEAR, RE)
            take(stage, NEAR, IM)
            arrived(stage, BACK, RE)
            take(stage, BACK, RE)

        @pl.when(has_far)
        def _():
            arrived(stage, FAR, IM)
            take_real(stage, FAR, IM)

        after = stage + 1
        more = stage < STAGES - 1

        def piece(half, begin=0):
            part = pl.ds(half * HALF, HALF)
            high, low = split(received(stage, BACK, IM, part))
            columns = [
                left_of[BACK, pl.ds(begin, M), pl.ds(block * M + half * HALF, HALF)]
                for block in range(3)
            ]
            return (
                jnp.concatenate(columns, axis=1),
                jnp.concatenate([high, high, low], axis=0),
                jnp.concatenate([high, high, low], axis=1),
                right_of[BACK, :, pl.ds(begin, M)],
            )

        def sides(half, begin):
            p_part, tall, wide, p_all = piece(half, begin)
            return (
                jnp.dot(p_part, tall, preferred_element_type=F32),
                jnp.dot(wide, p_all, preferred_element_type=F32),
            )

        top, bottom = pl.ds(0, HALF), pl.ds(HALF, HALF)

        def next_real(part, half, slope):
            total[1, part] = slope
            ybuf[after, RE, part] = ybuf[0, RE, part] + ahead * slope
            start(to_back_real(after, ybuf.at[after], half))
            if half == 0:
                far_real(after, ybuf.at[after])

        @pl.when(has_back & more)
        def _():
            arrived(stage, BACK, IM, 0)
            p_part, tall, wide, p_all = piece(0)
            total[1] += jnp.dot(p_part, tall, preferred_element_type=F32)
            total[1, top] -= jnp.dot(wide, p_all, preferred_element_type=F32)
            arrived(stage, BACK, IM, 1)
            p_part, tall, wide, p_all = piece(1)
            left = jnp.dot(p_part[:HALF], tall, preferred_element_type=F32)
            next_real(top, 0, total[1, top] + left)
            left = jnp.dot(p_part[HALF:], tall, preferred_element_type=F32)
            right = jnp.dot(wide, p_all, preferred_element_type=F32)
            next_real(bottom, 1, total[1, bottom] + (left - right))

        @pl.when(has_far & odd_one & jnp.logical_not(more))
        def _():
            take_rest(stage, FAR)

        def finish(half, complex_too):
            part = pl.ds(half * HALF, HALF)
            left, right = sides(half, 0)
            total[1] += left
            total[1, part] -= right
            if complex_too:
                left, right = sides(half, M)
                total[0] -= left
                total[0, part] -= right

        for half in (0, 1):
            @pl.when(has_back & jnp.logical_not(more))
            def _():
                arrived(stage, BACK, IM, half)

            @pl.when(has_back & even & jnp.logical_not(more))
            def _():
                finish(half, True)

            @pl.when(has_back & odd_one & jnp.logical_not(more))
            def _():
                finish(half, False)

        @pl.when(jnp.logical_not(has_back) & more)
        def _():
            ybuf[after, RE] = ybuf[0, RE] + ahead * total[1]
            far_real(after, ybuf.at[after])

        @pl.when(has_back & even & more)
        def _():
            take_rest(stage, BACK)

        @pl.when(has_far & odd_one & more)
        def _():
            take_rest(stage, FAR)

        @pl.when(stage < STAGES - 1)
        def _():
            ybuf[after, IM] = ybuf[0, IM] - ahead * total[0]
            start(to_sibling(after))

    def keep_real(after, ahead):
        zbuf[after, RE] = ybuf[0, RE] + ahead * total[1]

    def keep_imag(after, ahead):
        zbuf[after, IM] = ybuf[0, IM] - ahead * total[0]

    def take_rest(stage, slot):
        left, right = products(slot, received(stage, slot, IM), False, M)
        total[0] -= left + right

    def below_even(stage, ahead):
        after = stage + 1
        arrived(stage, NEAR, IM, 1)
        start(hand_imag(stage, 1))
        arrived(stage, FAR, RE, 0)
        start(hand_real(stage, 0))
        arrived(stage, FAR, RE, 1)
        start(hand_real(stage, 1))
        arrived(stage, NEAR, IM, 0)
        start(hand_imag(stage, 0))
        arrived(stage, NEAR, RE)
        take_complex(stage, NEAR, RE)
        take_complex(stage, NEAR, IM)
        arrived(stage, BACK, RE)
        take_complex(stage, BACK, RE)
        arrived(stage, BACK, IM, 0)
        arrived(stage, BACK, IM, 1)
        take_real(stage, BACK, IM)

        @pl.when(stage < STAGES - 1)
        def _():
            keep_real(after, ahead)
            start(to_far_real(after, zbuf.at[after]))

        take_rest(stage, BACK)

        @pl.when(stage < STAGES - 1)
        def _():
            keep_imag(after, ahead)

        take_real(stage, FAR, RE)
        arrived(stage, FAR, IM)
        take_real(stage, FAR, IM)

        @pl.when(stage < STAGES - 1)
        def _():
            ybuf[after, RE] = ybuf[0, RE] + ahead * total[1]
            start(to_back_real(after, ybuf.at[after], 0))
            start(to_back_real(after, ybuf.at[after], 1))
            ybuf[after, IM] = ybuf[0, IM] - ahead * total[0]
            start(to_sibling(after))

    def below_odd(stage, ahead):
        after = stage + 1
        arrived(stage, FAR, RE, 0)
        start(hand_real(stage, 0))
        arrived(stage, FAR, RE, 1)
        start(hand_real(stage, 1))
        take_complex(stage, FAR, RE)
        arrived(stage, NEAR, IM, 1)
        start(hand_imag(stage, 1))
        arrived(stage, NEAR, IM, 0)
        start(hand_imag(stage, 0))
        arrived(stage, FAR, IM)
        take_real(stage, FAR, IM)

        @pl.when(stage < STAGES - 1)
        def _():
            keep_real(after, ahead)
            start(to_back_real(after, zbuf.at[after], 0))
            start(to_back_real(after, zbuf.at[after], 1))

        take_rest(stage, FAR)

        @pl.when(stage < STAGES - 1)
        def _():
            keep_imag(after, ahead)
            part_to_sibling(after).start()

        take_real(stage, NEAR, IM)
        arrived(stage, NEAR, RE)
        take_real(stage, NEAR, RE)
        arrived(stage, BACK, RE)
        take_real(stage, BACK, RE)
        arrived(stage, BACK, IM, 0)
        arrived(stage, BACK, IM, 1)
        take_real(stage, BACK, IM)

        @pl.when(stage < STAGES - 1)
        def _():
            ybuf[after, RE] = ybuf[0, RE] + ahead * total[1]
            start(to_far_real(after, ybuf.at[after]))
            ybuf[after, IM] = ybuf[0, IM] - ahead * total[0]
            start(to_sibling(after))

    def late_below(stage):
        @pl.when(even)
        def _():
            part_to_sibling(stage).wait_recv()
            start(to_far_late(stage, zbuf.at[stage], zsib.at[stage]))
            arrived(stage, SIB, IM)

        @pl.when(odd_one)
        def _():
            arrived(stage, SIB, IM)
            start(to_far_late(stage, ybuf.at[stage], win.at[stage, SIB, IM]))

    def stage_body(stage, carry):
        arrived(stage, SIB, RE)
        take(stage, SIB, RE)
        take(stage, SIB, IM)

        @pl.when(above & (stage < STAGES - 1))
        def _():
            contribute(stage)

        ahead = jnp.where(stage == 2, STEP, STEP / 2).astype(F32)

        @pl.when(jnp.logical_not(below))
        def _():
            usual(stage, ahead)

        @pl.when(below & even)
        def _():
            below_even(stage, ahead)

        @pl.when(below & odd_one)
        def _():
            below_odd(stage, ahead)

        @pl.when(stage < STAGES - 1)
        def _():
            weight = jnp.where(stage == 0, 1.0, 2.0).astype(F32)
            acc[RE] += weight * total[1]
            acc[IM] -= weight * total[0]
            own_products(stage + 1, (RE,))

        @pl.when((stage < STAGES - 1) & jnp.logical_not(below))
        def _():
            send_late(stage + 1)

        @pl.when((stage < STAGES - 1) & below)
        def _():
            late_below(stage + 1)

        @pl.when(stage < STAGES - 1)
        def _():
            own_products(stage + 1, (IM,))

        return carry

    lax.fori_loop(0, STAGES, stage_body, 0)

    out[0, RE] = ybuf[0, RE] + (STEP / 6) * (acc[RE] + total[1])
    out[0, IM] = ybuf[0, IM] + (STEP / 6) * (acc[IM] - total[0])

    sent(ybuf, send_sem.at[TO_SIB])

    @pl.when(has_back)
    def _():
        sent(ybuf, send_sem.at[TO_BACK])

    @pl.when(has_far)
    def _():
        sent(win.at[pl.ds(0, 2)], send_sem.at[TO_FAR])

    @pl.when(below & odd_one)
    def _():
        sent(zsib.at[pl.ds(0, STAGES - 1)], z_send)

    @pl.when(below & even)
    def _():
        rim_row(1, FAR).wait_send()

    @pl.when(below & odd_one)
    def _():
        rim_row(0, NEAR).wait_send()
        rim_row(0, BACK).wait_send()


def on_device(
    state, h_static, drive_op, couple, bath_coef, damping, occupation, raise_nbr, lower_nbr
):
    count = lax.axis_size("aux")
    return pl.pallas_call(
        functools.partial(kernel, count),
        out_shape=jax.ShapeDtypeStruct(state.shape, F32),
        in_specs=[pl.BlockSpec(memory_space=pltpu.HBM)] * 9,
        out_specs=pl.BlockSpec(memory_space=pltpu.VMEM),
        scratch_shapes=[
            pltpu.SMEM((2, MODES), F32),
            pltpu.SMEM((MODES,), F32),
            pltpu.SMEM((1, MODES), jnp.int32),
            pltpu.SMEM((1, MODES), jnp.int32),
            pltpu.SMEM((1, MODES), jnp.int32),
            pltpu.VMEM((STAGES, 2, M, M), F32),
            pltpu.VMEM((STAGES, 4, 2, M, M), F32),
            pltpu.VMEM((7, M, M), F32),
            pltpu.VMEM((2, 2, M, M), F32),
            pltpu.VMEM((OWN + 3, 2 * M, 3 * M), BF),
            pltpu.VMEM((OWN + 3, 3 * M, 2 * M), BF),
            pltpu.VMEM((2, M, M), F32),
            pltpu.VMEM((2, M, M), F32),
            pltpu.SMEM((2, 1, MODES), jnp.int32),
            pltpu.VMEM((STAGES, 2, M, M), F32),
            pltpu.VMEM((STAGES, M, M), F32),
            pltpu.VMEM((3, M, 3 * M), BF),
            pltpu.VMEM((3, 3 * M, M), BF),
            pltpu.VMEM((2, 2, 2, M, M), F32),
            pltpu.SemaphoreType.DMA((7,)),
            pltpu.SemaphoreType.DMA((3,)),
            pltpu.SemaphoreType.DMA((3, 9)),
            pltpu.SemaphoreType.DMA((2, 2)),
            pltpu.SemaphoreType.DMA((2,)),
            pltpu.SemaphoreType.DMA((2,)),
            pltpu.SemaphoreType.DMA,
            pltpu.SemaphoreType.DMA((STAGES - 1,)),
        ],
        compiler_params=pltpu.CompilerParams(
            collective_id=0, has_side_effects=True, vmem_limit_bytes=48 << 20
        ),
        name="rk_step",
    )(
        *(
            pltpu.with_memory_space_constraint(x, pltpu.HBM)
            for x in (
                bath_coef,
                damping,
                occupation,
                raise_nbr,
                lower_nbr,
                state,
                h_static,
                drive_op,
                couple,
            )
        )
    )


def solution(mesh):
    return jax.shard_map(
        on_device,
        mesh=mesh,
        in_specs=(
            P("aux", None, None, None),
            P(),
            P(),
            P(),
            P(),
            P(),
            P("aux", None),
            P("aux", None),
            P("aux", None),
        ),
        out_specs=P("aux", None, None, None),
        check_vma=False,
    )
```
